128 devices in a mesh: blk: 16 (over z, y), group: 8 (over x, core).
Axes of the slice: x: 4, y: 4, z: 4, core: 2. Of those that a mesh axis runs over, the one named last changes fastest.
Arguments:
- hidden: bfloat16 [8, 2048, 2048], P('group', 'blk'), may hold values from -6 to 6
- cache_len: int32 [8], P('group'), may hold values from 0 to 2048, as said below
- cache_kv: bfloat16 [8, 2048, 8, 128], P('group', 'blk'), may hold values from -6 to 6
- norm_gain: float32 [2048], replicated, may hold values from 0.5 to 1.5
- w_query: bfloat16 [2048, 2048], replicated, may hold values from -0.125 to 0.125
- w_key: bfloat16 [2048, 512], replicated, may hold values from -0.125 to 0.125
- w_value: bfloat16 [2048, 512], replicated, may hold values from -0.125 to 0.125
- q_gain: float32 [32, 64], replicated, may hold values from 0.25 to 13.5
- k_gain: float32 [8, 64], replicated, may hold values from 0.3 to 6.5
- w_out: bfloat16 [2048, 2048], replicated, may hold values from -0.5 to 0.5
Outputs:
- projected: bfloat16 [8, 2048, 2048], P('group', 'blk')
- new_cache: bfloat16 [8, 2048, 8, 128], P(None, 'blk', 'group')
The draws below stay inside these ranges and needn't reach their ends.
Inputs may be any that keep to these rules, and one draw needn't show every extreme that they name: `cache_len`: some request has exactly 2048 live cache slots.
All inputs are finite; a program needn't handle non-finite values.
Results may differ from the reference program's by a relative error of at most 0.04.
Values may be sent and summed in bfloat16 or wider, within the bound.
A program may use at most 192 MiB of HBM per device.

```python
import math
import jax
import jax.numpy as jnp
from jax import lax

D = 2048
HEADS = 32
KVH = 8
HD = 64
TOK_DEV = 128
STRETCH = 2048
CACHE = 2048
GROUPS = 8
N_BLK = 16


def draw_cache_len(key, part):
    length_key, place_key = jax.random.split(key)
    lengths = jax.random.randint(length_key, (GROUPS,), 0, CACHE + 1, dtype=jnp.int32)
    chosen = jax.random.randint(place_key, (), 0, GROUPS, dtype=jnp.int32)
    return jnp.where(jnp.arange(GROUPS, dtype=jnp.int32) == chosen, CACHE, lengths).astype(jnp.int32)


def head_gains(key, head_count, lowest, highest):
    head_key, entry_key = jax.random.split(key)
    level = jnp.exp(jax.random.uniform(head_key, (head_count, 1), jnp.float32, math.log(lowest), math.log(highest)))
    ripple = 1.0 + 0.1 * jnp.clip(jax.random.normal(entry_key, (head_count, HD), jnp.float32), -3.0, 3.0)
    return (level * ripple).astype(jnp.float32)


def draw_q_gain(key, part):
    return head_gains(jax.random.fold_in(key, 11), HEADS, 1.0, 3.0)


def draw_k_gain(key, part):
    return head_gains(jax.random.fold_in(key, 23), KVH, 0.8, 1.25)


def steps_of(key, extent, pieces, low, largest):
    level = 1.0
    for dim, blocks in pieces:
        draws = jax.random.uniform(jax.random.fold_in(jax.random.fold_in(key, 6), dim), (blocks,), jnp.float32, low / len(pieces), largest / len(pieces))
        level = level * jnp.repeat(jnp.exp(draws), extent[dim] // blocks).reshape((-1,) + (1,) * (len(extent) - 1 - dim))
    return level


def normal_values(rng, shape, deviation, bound, cuts=(), held_as=jnp.bfloat16):
    entries = deviation * jax.random.normal(rng, shape, jnp.float32)
    if cuts:
        entries = entries * steps_of(rng, shape, cuts, -0.22, 0.18)
    return jnp.clip(entries, -bound, bound).astype(held_as)


def setup_inputs(seed: int = 0) -> dict:
    seeds = jax.random.split(jax.random.key(seed), 11)
    hidden = normal_values(seeds[0], (GROUPS, STRETCH, D), 1.0, 6.0, ((0, 8), (1, 16)))
    cache_len = draw_cache_len(jax.random.fold_in(seeds[10], 71), 0)
    cache_kv = normal_values(seeds[2], (GROUPS, CACHE, KVH, 2 * HD), 1.0, 6.0, ((0, 8), (1, 16)))
    norm_gain = jnp.clip(1.0 + 0.1 * jax.random.normal(seeds[3], (D,), jnp.float32), 0.5, 1.5)
    w_query = normal_values(seeds[4], (D, D), D ** -0.5, 0.125)
    w_key = normal_values(seeds[5], (D, KVH * HD), D ** -0.5, 0.125)
    w_value = normal_values(seeds[6], (D, KVH * HD), D ** -0.5, 0.125)
    q_gain = draw_q_gain(jax.random.fold_in(seeds[10], 71), 0)
    k_gain = draw_k_gain(jax.random.fold_in(seeds[10], 71), 0)
    w_out = normal_values(seeds[9], (D, D), (D // 16) ** -0.5, 0.5)
    return {"hidden": hidden, "cache_len": cache_len, "cache_kv": cache_kv, "norm_gain": norm_gain, "w_query": w_query, "w_key": w_key, "w_value": w_value, "q_gain": q_gain, "k_gain": k_gain, "w_out": w_out}


EPSILON = 1e-05
THETA = 1000000.0

def mirrored(owner_block, within, per_block, blocks):
    half_block = per_block // 2
    return jnp.where(within < half_block, owner_block * half_block + within, (2 * blocks - 1 - owner_block) * half_block + within - half_block)

def rms_scale(values, gain_row):
    return values * lax.rsqrt(lax.optimization_barrier(jnp.mean(values * values, axis=-1, keepdims=True)) + EPSILON) * gain_row

def rotary(values, position):
    half_dim = values.shape[-1] // 2
    inverse = THETA ** (-jnp.arange(half_dim, dtype=jnp.float32) * 2.0 / values.shape[-1])
    angles = position.astype(jnp.float32)[:, None] * inverse[None, :]
    cos_values = jnp.cos(angles)[:, None, :]
    sine_values = jnp.sin(angles)[:, None, :]
    front_half = values[..., :half_dim]
    back_half = values[..., half_dim:]
    return jnp.concatenate([front_half * cos_values - back_half * sine_values, back_half * cos_values + front_half * sine_values], -1)

def reference(hidden, cache_len, cache_kv, norm_gain, w_query, w_key, w_value, q_gain, k_gain, w_out):
    head_count, head_dim = q_gain.shape
    kv_heads = k_gain.shape[0]
    per_group = head_count // kv_heads
    row_index = jnp.arange(STRETCH, dtype=jnp.int32)
    new_pos = mirrored(row_index // TOK_DEV, row_index % TOK_DEV, TOK_DEV, N_BLK).astype(jnp.int32)
    cache_index = jnp.arange(CACHE, dtype=jnp.int32)
    outputs = []
    caches = []
    for group_index in range(GROUPS):
        length = cache_len[group_index]
        floats = hidden[group_index].astype(jnp.float32)
        normed = rms_scale(floats, norm_gain).astype(jnp.bfloat16)
        query_rows = jnp.dot(normed, w_query, preferred_element_type=jnp.float32).reshape(STRETCH, head_count, head_dim)
        key_rows = jnp.dot(normed, w_key, preferred_element_type=jnp.float32).reshape(STRETCH, kv_heads, head_dim)
        value_rows = jnp.dot(normed, w_value, preferred_element_type=jnp.float32).reshape(STRETCH, kv_heads, head_dim)
        query_rows = rotary(rms_scale(query_rows, q_gain), length + new_pos).astype(jnp.bfloat16)
        key_rows = rotary(rms_scale(key_rows, k_gain), length + new_pos).astype(jnp.bfloat16)
        value_rows = value_rows.astype(jnp.bfloat16)
        new_entries = jnp.concatenate([key_rows, value_rows], -1)
        every_key = jnp.concatenate([cache_kv[group_index], new_entries], 0)
        visible = jnp.concatenate([jnp.broadcast_to((cache_index < length)[None, :], (STRETCH, CACHE)), new_pos[None, :] <= new_pos[:, None]], 1)
        query_heads = query_rows.reshape(STRETCH, kv_heads, per_group, head_dim).transpose(1, 2, 0, 3)
        key_heads = every_key.transpose(1, 0, 2)

        def one_head(operands):
            query_head, key_value = operands
            scores = jnp.einsum('gtd,nd->gtn', query_head.astype(jnp.float32), key_value[:, :head_dim].astype(jnp.float32)) * 0.125
            scores = jnp.where(visible[None], scores, -1e+30)
            row_max = lax.optimization_barrier(jnp.max(scores, -1, keepdims=True))
            exp_terms = jnp.where(visible[None], jnp.exp(scores - row_max), 0.0)
            denominator = lax.optimization_barrier(jnp.sum(exp_terms, -1))
            weights = exp_terms.astype(jnp.bfloat16)
            summed = jnp.einsum('gtn,nd->gtd', weights.astype(jnp.float32), key_value[:, head_dim:].astype(jnp.float32))
            return summed / denominator[..., None]
        attended = lax.map(one_head, (query_heads, key_heads))
        attended_rows = attended.transpose(2, 0, 1, 3).reshape(STRETCH, head_count * head_dim).astype(jnp.bfloat16)
        outputs.append(jnp.dot(attended_rows, w_out, preferred_element_type=jnp.float32).astype(jnp.bfloat16))
        caches.append(new_entries)
    return (jnp.stack(outputs), jnp.stack(caches))
```

```python
import functools, math
import jax, jax.numpy as jnp
from jax import lax
from jax.experimental import pallas as pl
from jax.experimental.pallas import tpu as pltpu
F32, BF16 = jnp.float32, jnp.bfloat16
NEG = -1e30

def prep_keys(src, row0, rows, length, kt_ref, vo_ref):
    x = src.astype(F32)
    lane = lax.broadcasted_iota(jnp.int32, x.shape, 1)
    if length is None:
        bias = jnp.zeros_like(x)
    else:
        row = lax.broadcasted_iota(jnp.int32, x.shape, 0) + row0
        bias = jnp.where(row < length, 0.0, NEG)
    k = jnp.where(lane < 64, x, bias)
    kt_ref[:, pl.ds(row0, rows)] = k.T.astype(BF16)
    vo_ref[pl.ds(row0, rows), :] = jnp.where(lane < 64, 1.0, x).astype(BF16)

def prep_q(src, qs_ref, i):
    x = src.astype(F32)
    lane = lax.broadcasted_iota(jnp.int32, x.shape, 1)
    tail = jnp.where(lane == 64, 1.0, 0.0)
    qs_ref[i, 0:256, :] = jnp.where(lane < 64, x, tail).astype(BF16)
    qs_ref[i, 256:512, :] = jnp.where(lane < 64, pltpu.roll(x, 64, 1), tail).astype(BF16)

KB = 512
def attend(qs_ref, kt_ref, vo_ref, s0, s1, mx0, mx1, acc, emit):
    ncache = 2048 // KB
    def qk(i, c, s, mx, first=False, diag=None):
        off = pl.multiple_of(c * KB, KB)
        sc = jnp.dot(qs_ref[i], kt_ref[:, pl.ds(off, KB)], preferred_element_type=F32)
        if diag is not None:
            r = lax.broadcasted_iota(jnp.int32, (512, KB), 0)
            r = jnp.where(r >= 256, r - 256, r) + diag * 256
            col = lax.broadcasted_iota(jnp.int32, (512, KB), 1)
            sc = jnp.where(col <= r, sc, NEG)
        s[:, pl.ds(off, KB)] = sc
        mm = sc[:, 0:128]
        for l in range(1, KB // 128):
            mm = jnp.maximum(mm, sc[:, l * 128:(l + 1) * 128])
        mx[...] = jnp.maximum(mx[...], mm)
    def pv(c, s, mx):
        off = pl.multiple_of(c * KB, KB)
        m = mx[...]
        p = jnp.exp2(s[:, pl.ds(off, KB)] - jnp.concatenate([m] * (KB // 128), 1)).astype(BF16)
        acc[...] += jnp.dot(p, vo_ref[pl.ds(off, KB), :], preferred_element_type=F32)
    def start(mx):
        mx[...] = jnp.full(mx.shape, NEG, F32)
    def finish_max(mx):
        mx[...] = jnp.broadcast_to(jnp.max(mx[...], 1, keepdims=True), mx.shape)
    def out(i):
        a = acc[...]
        lane = lax.broadcasted_iota(jnp.int32, (256, 128), 1)
        h0, h1 = a[0:256], a[256:512]
        num = jnp.where(lane < 64, pltpu.roll(h0, 64, 1), h1)
        den = jnp.where(lane < 64, h0, pltpu.roll(h1, 64, 1))
        emit(i, (num / den).astype(BF16))
        acc[...] = jnp.zeros(acc.shape, F32)
    acc[...] = jnp.zeros(acc.shape, F32)
    start(mx0)
    for c in range(ncache):
        qk(0, c, s0, mx0)
    qk(0, ncache, s0, mx0, diag=0)
    finish_max(mx0)
    def pair(t, _):
        last = ncache + t
        start(mx1)
        def a(c, _):
            qk(2 * t + 1, c, s1, mx1); pv(c, s0, mx0); return 0
        lax.fori_loop(0, last, a, 0)
        qk(2 * t + 1, last, s1, mx1, diag=1); pv(last, s0, mx0)
        finish_max(mx1); out(2 * t)
        start(mx0)
        def b(c, _):
            qk(2 * t + 2, c, s0, mx0); pv(c, s1, mx1); return 0
        lax.fori_loop(0, last + 1, b, 0)
        qk(2 * t + 2, last + 1, s0, mx0, diag=0)
        finish_max(mx0); out(2 * t + 1)
        return 0
    npair = 4
    lax.fori_loop(0, npair - 1, pair, 0)
    t = npair - 1; last = ncache + t
    start(mx1)
    def a(c, _):
        qk(2 * t + 1, c, s1, mx1); pv(c, s0, mx0); return 0
    lax.fori_loop(0, last, a, 0)
    qk(2 * t + 1, last, s1, mx1, diag=1); pv(last, s0, mx0)
    finish_max(mx1); out(2 * t)
    def fin(c, _):
        pv(c, s1, mx1); return 0
    lax.fori_loop(0, last + 1, fin, 0)
    out(2 * t + 1)

SCRATCH = [pltpu.VMEM((8, 512, 128), BF16), pltpu.VMEM((128, 4096), BF16), pltpu.VMEM((4096, 128), BF16),
    pltpu.VMEM((512, 4096), F32), pltpu.VMEM((512, 4096), F32), pltpu.VMEM((512, 128), F32), pltpu.VMEM((512, 128), F32), pltpu.VMEM((512, 128), F32)]

def kernel(len_ref, q_ref, kv_ref, o_ref, qs, kt, vo, s0, s1, mx0, mx1, acc):
    length = len_ref[0]
    for b in range(16):
        prep_keys(kv_ref[b, 0:128], b * 128, 128, length, kt, vo)
    for i in range(16):
        p = 2 * i
        rows = [kv_ref[c, 128:192] if c < 16 else kv_ref[31 - c, 192:256] for c in (p, p + 1)]
        prep_keys(jnp.concatenate(rows, 0), 2048 + i * 128, 128, None, kt, vo)
    for i in range(8):
        rows = [q_ref[c, 0:64] if c < 16 else q_ref[31 - c, 64:128] for c in range(4 * i, 4 * i + 4)]
        prep_q(jnp.concatenate(rows, 0), qs, i)
    def emit(i, val):
        o_ref[pl.ds(i * 256, 256), :] = val
    attend(qs, kt, vo, s0, s1, mx0, mx1, acc, emit)

def attention(length, q, kv):
    return pl.pallas_call(kernel, out_shape=jax.ShapeDtypeStruct((2048, 128), BF16),
        in_specs=[pl.BlockSpec(memory_space=pltpu.SMEM), pl.BlockSpec(memory_space=pltpu.VMEM), pl.BlockSpec(memory_space=pltpu.VMEM)],
        out_specs=pl.BlockSpec(memory_space=pltpu.VMEM), scratch_shapes=SCRATCH,
        compiler_params=pltpu.CompilerParams(vmem_limit_bytes=60 << 20), name="attend")(length, q, kv)

EPS=1e-5; THETA=1e6
QSCALE = 0.125 * math.log2(math.e)

def rope_tables(pos_f):
    lane = lax.broadcasted_iota(jnp.int32, (1, 128), 1)
    inv = jnp.exp(lax.rem(lane, 32).astype(F32) * (-2.0 / 64.0 * math.log(THETA)))
    ang = pos_f * inv
    sgn = jnp.where(lax.rem(lane, 64) < 32, -1.0, 1.0)
    return jnp.cos(ang), jnp.sin(ang) * sgn

def norm_rows(hid, gain):
    x = hid.astype(F32)
    return (x * lax.rsqrt(jnp.mean(x * x, -1, keepdims=True) + EPS) * gain).astype(BF16)

def block_ones():
    a = lax.broadcasted_iota(jnp.int32, (128, 128), 0) // 64
    b = lax.broadcasted_iota(jnp.int32, (128, 128), 1) // 64
    return jnp.where(a == b, 1.0, 0.0).astype(BF16)

def head_rope(x, gain, cos, sin, ones):
    sq = x * x
    hi = sq.astype(BF16)
    lo = (sq - hi.astype(F32)).astype(BF16)
    tot = jnp.dot(hi, ones, preferred_element_type=F32) + jnp.dot(lo, ones, preferred_element_type=F32)
    n = x * lax.rsqrt(tot * (1.0 / 64) + EPS) * gain
    lane = lax.broadcasted_iota(jnp.int32, n.shape, 1)
    sw = jnp.where(lax.rem(lane, 64) < 32, pltpu.roll(n, 96, 1), pltpu.roll(n, 32, 1))
    return n * cos + sw * sin

def pair_gain(g_ref, j):
    return jnp.concatenate([g_ref[2 * j:2 * j + 1, :], g_ref[2 * j + 1:2 * j + 2, :]], 1)

def proj_kernel(len_ref, hid_ref, ng_ref, qg_ref, kg_ref, wk_hbm, wv_hbm, wq_hbm, q_ref, kv_ref, w, normed, sem):
    copies = []
    for n, (src, off) in enumerate([(wk_hbm, 0), (wv_hbm, 0)] + [(wq_hbm, 512 * i) for i in range(4)]):
        cp = pltpu.make_async_copy(src.at[:, pl.ds(off, 512)], w.at[n], sem.at[n])
        cp.start(); copies.append(cp)
    b = lax.axis_index("blk")
    j = lax.broadcasted_iota(jnp.int32, (128, 1), 0)
    pos = jnp.where(j < 64, b * 64 + j, (31 - b) * 64 + j - 64) + len_ref[0]
    cos, sin = rope_tables(pos.astype(F32))
    normed[...] = norm_rows(hid_ref[...], ng_ref[...])
    ones = block_ones()
    lane = lax.broadcasted_iota(jnp.int32, (128, 128), 1)
    copies[0].wait(); copies[1].wait()
    k = jnp.dot(normed[...], w[0], preferred_element_type=F32)
    v = jnp.dot(normed[...], w[1], preferred_element_type=F32)
    for t in range(4):
        kk = head_rope(k[:, t * 128:(t + 1) * 128], pair_gain(kg_ref, t), cos, sin, ones)
        vv = v[:, t * 128:(t + 1) * 128]
        kv_ref[2 * t] = jnp.where(lane < 64, kk, pltpu.roll(vv, 64, 1)).astype(BF16)
        kv_ref[2 * t + 1] = jnp.where(lane < 64, pltpu.roll(kk, 64, 1), vv).astype(BF16)
    cosq, sinq = cos * QSCALE, sin * QSCALE
    for c in range(4):
        copies[2 + c].wait()
        q = jnp.dot(normed[...], w[2 + c], preferred_element_type=F32)
        for t in range(4):
            q_ref[4 * c + t] = head_rope(q[:, t * 128:(t + 1) * 128], pair_gain(qg_ref, 4 * c + t), cosq, sinq, ones).astype(BF16)

def project(length, hid, ng, qg, kg, wk, wv, wq):
    vm = pl.BlockSpec(memory_space=pltpu.VMEM); hb = pl.BlockSpec(memory_space=pl.ANY)
    return pl.pallas_call(proj_kernel, out_shape=(jax.ShapeDtypeStruct((16, 128, 128), BF16), jax.ShapeDtypeStruct((8, 128, 128), BF16)),
        in_specs=[pl.BlockSpec(memory_space=pltpu.SMEM), vm, vm, vm, vm, hb, hb, hb], out_specs=(vm, vm),
        scratch_shapes=[pltpu.VMEM((6, 2048, 512), BF16), pltpu.VMEM((128, 2048), BF16), pltpu.SemaphoreType.DMA((6,))],
        compiler_params=pltpu.CompilerParams(vmem_limit_bytes=40 << 20), name="project")(length, hid, ng, qg, kg, wk, wv, wq)

def shards(hidden, cache_len, cache_kv, norm_gain, w_query, w_key, w_value, q_gain, k_gain, w_out):
    q, new = project(cache_len, hidden[0], norm_gain[None], q_gain, k_gain, w_key, w_value, w_query)
    kv = jnp.concatenate([cache_kv[0].transpose(1, 0, 2), new], 1)
    kv = jnp.repeat(kv, 2, axis=0)
    kv = lax.all_to_all(kv, "blk", split_axis=0, concat_axis=0, tiled=True)
    q = lax.all_to_all(q, "blk", split_axis=0, concat_axis=0, tiled=True)
    dec = lax.all_to_all(new, "group", split_axis=0, concat_axis=0, tiled=True)[:, :, None, :]
    o = attention(cache_len, q, kv).reshape(32, 64, 128)
    o = jnp.concatenate([o[:16], o[16:][::-1]], 1)
    o = lax.all_to_all(o, "blk", split_axis=0, concat_axis=0, tiled=True)
    o = o.transpose(1, 0, 2).reshape(128, 2048)
    return jnp.dot(o, w_out, preferred_element_type=F32).astype(BF16)[None], dec


def solution(mesh):
    from jax.sharding import PartitionSpec as P
    in_specs = (P("group", "blk", None), P("group"), P("group", "blk", None, None)) + (P(),) * 7
    out_specs = (P("group", "blk", None), P(None, "blk", "group", None))
    return jax.shard_map(shards, mesh=mesh, in_specs=in_specs, out_specs=out_specs, check_vma=False)
```

```python
import functools, math
import jax, jax.numpy as jnp
from jax import lax
from jax.experimental import pallas as pl
from jax.experimental.pallas import tpu as pltpu
F32, BF16 = jnp.float32, jnp.bfloat16
NEG = -1e30

def prep_keys(src, row0, rows, length, kt_ref, vo_ref):
    x = src.astype(F32)
    lane = lax.broadcasted_iota(jnp.int32, x.shape, 1)
    if length is None:
        bias = jnp.zeros_like(x)
    else:
        row = lax.broadcasted_iota(jnp.int32, x.shape, 0) + row0
        bias = jnp.where(row < length, 0.0, NEG)
    k = jnp.where(lane < 64, x, bias)
    kt_ref[:, pl.ds(row0, rows)] = k.T.astype(BF16)
    vo_ref[pl.ds(row0, rows), :] = jnp.where(lane < 64, 1.0, x).astype(BF16)

def prep_q(src, qs_ref, i):
    x = src.astype(F32)
    lane = lax.broadcasted_iota(jnp.int32, x.shape, 1)
    tail = jnp.where(lane == 64, 1.0, 0.0)
    qs_ref[i, 0:256, :] = jnp.where(lane < 64, x, tail).astype(BF16)
    qs_ref[i, 256:512, :] = jnp.where(lane < 64, pltpu.roll(x, 64, 1), tail).astype(BF16)

KB = 512
def attend(qs_ref, kt_ref, vo_ref, s0, s1, mx0, mx1, acc, emit):
    ncache = 2048 // KB
    def qk(i, c, s, mx, first=False, diag=None):
        off = pl.multiple_of(c * KB, KB)
        sc = jnp.dot(qs_ref[i], kt_ref[:, pl.ds(off, KB)], preferred_element_type=F32)
        if diag is not None:
            r = lax.broadcasted_iota(jnp.int32, (512, KB), 0)
            r = jnp.where(r >= 256, r - 256, r) + diag * 256
            col = lax.broadcasted_iota(jnp.int32, (512, KB), 1)
            sc = jnp.where(col <= r, sc, NEG)
        s[:, pl.ds(off, KB)] = sc
        mm = sc[:, 0:128]
        for l in range(1, KB // 128):
            mm = jnp.maximum(mm, sc[:, l * 128:(l + 1) * 128])
        mx[...] = jnp.maximum(mx[...], mm)
    def pv(c, s, mx):
        off = pl.multiple_of(c * KB, KB)
        m = mx[...]
        p = jnp.exp2(s[:, pl.ds(off, KB)] - jnp.concatenate([m] * (KB // 128), 1)).astype(BF16)
        acc[...] += jnp.dot(p, vo_ref[pl.ds(off, KB), :], preferred_element_type=F32)
    def start(mx):
        mx[...] = jnp.full(mx.shape, NEG, F32)
    def finish_max(mx):
        mx[...] = jnp.broadcast_to(jnp.max(mx[...], 1, keepdims=True), mx.shape)
    def out(i):
        a = acc[...]
        lane = lax.broadcasted_iota(jnp.int32, (256, 128), 1)
        h0, h1 = a[0:256], a[256:512]
        num = jnp.where(lane < 64, pltpu.roll(h0, 64, 1), h1)
        den = jnp.where(lane < 64, h0, pltpu.roll(h1, 64, 1))
        emit(i, (num / den).astype(BF16))
        acc[...] = jnp.zeros(acc.shape, F32)
    acc[...] = jnp.zeros(acc.shape, F32)
    start(mx0)
    for c in range(ncache):
        qk(0, c, s0, mx0)
    qk(0, ncache, s0, mx0, diag=0)
    finish_max(mx0)
    def pair(t, _):
        last = ncache + t
        start(mx1)
        def a(c, _):
            qk(2 * t + 1, c, s1, mx1); pv(c, s0, mx0); return 0
        lax.fori_loop(0, last, a, 0)
        qk(2 * t + 1, last, s1, mx1, diag=1); pv(last, s0, mx0)
        finish_max(mx1); out(2 * t)
        start(mx0)
        def b(c, _):
            qk(2 * t + 2, c, s0, mx0); pv(c, s1, mx1); return 0
        lax.fori_loop(0, last + 1, b, 0)
        qk(2 * t + 2, last + 1, s0, mx0, diag=0)
        finish_max(mx0); out(2 * t + 1)
        return 0
    npair = 4
    lax.fori_loop(0, npair - 1, pair, 0)
    t = npair - 1; last = ncache + t
    start(mx1)
    def a(c, _):
        qk(2 * t + 1, c, s1, mx1); pv(c, s0, mx0); return 0
    lax.fori_loop(0, last, a, 0)
    qk(2 * t + 1, last, s1, mx1, diag=1); pv(last, s0, mx0)
    finish_max(mx1); out(2 * t)
    def fin(c, _):
        pv(c, s1, mx1); return 0
    lax.fori_loop(0, last + 1, fin, 0)
    out(2 * t + 1)

EPS=1e-5; THETA=1e6
QSCALE = 0.125 * math.log2(math.e)

def rope_tables(pos_f):
    lane = lax.broadcasted_iota(jnp.int32, (1, 128), 1)
    inv = jnp.exp(lax.rem(lane, 32).astype(F32) * (-2.0 / 64.0 * math.log(THETA)))
    ang = pos_f * inv
    sgn = jnp.where(lax.rem(lane, 64) < 32, -1.0, 1.0)
    return jnp.cos(ang), jnp.sin(ang) * sgn

def norm_rows(hid, gain):
    x = hid.astype(F32)
    return (x * lax.rsqrt(jnp.mean(x * x, -1, keepdims=True) + EPS) * gain).astype(BF16)

def block_ones():
    a = lax.broadcasted_iota(jnp.int32, (128, 128), 0) // 64
    b = lax.broadcasted_iota(jnp.int32, (128, 128), 1) // 64
    return jnp.where(a == b, 1.0, 0.0).astype(BF16)

def head_rope(x, gain, cos, sin, ones):
    sq = x * x
    hi = sq.astype(BF16)
    lo = (sq - hi.astype(F32)).astype(BF16)
    tot = jnp.dot(hi, ones, preferred_element_type=F32) + jnp.dot(lo, ones, preferred_element_type=F32)
    n = x * lax.rsqrt(tot * (1.0 / 64) + EPS) * gain
    lane = lax.broadcasted_iota(jnp.int32, n.shape, 1)
    sw = jnp.where(lax.rem(lane, 64) < 32, pltpu.roll(n, 96, 1), pltpu.roll(n, 32, 1))
    return n * cos + sw * sin

def pair_gain(g_ref, j):
    return jnp.concatenate([g_ref[2 * j:2 * j + 1, :], g_ref[2 * j + 1:2 * j + 2, :]], 1)

def remote(src, dst, ssem, rsem, dev):
    return pltpu.make_async_remote_copy(src_ref=src, dst_ref=dst, send_sem=ssem, recv_sem=rsem,
                                        device_id=dev, device_id_type=pl.DeviceIdType.MESH)

def layer_kernel(len_ref, hid_ref, cache_ref, ng_ref, qg_ref, kg_ref, wk_hbm, wv_hbm, wq_hbm, wo_hbm, out_ref, dec_ref,
                 w, wo, normed, kvnew, qsend, kvc, kvn, qrecv, osend, orecv, oall, qs, kt, vo, s0, s1, mx0, mx1, acc,
                 wsem, wosem, c_ss, c_rs, n_ss, n_rs, q_ss, q_rs, d_ss, d_rs, o_ss, o_rs):
    b = lax.axis_index("blk"); g = lax.axis_index("group")
    def col(n):
        return pl.ds(pl.multiple_of(n * 512, 512), 512)
    plane = [(b // 4 + 1 + c) % 4 for c in range(4)]
    copies = [pltpu.make_async_copy(wk_hbm, w.at[0], wsem.at[0]), pltpu.make_async_copy(wv_hbm, w.at[1], wsem.at[1])]
    copies += [pltpu.make_async_copy(wq_hbm.at[:, col(plane[c])], w.at[2 + c], wsem.at[2 + c]) for c in range(4)]
    for cp in copies:
        cp.start()
    barrier = pltpu.get_barrier_semaphore()
    def hello(r, _):
        pl.semaphore_signal(barrier, inc=1, device_id=((b + r) % 16, g), device_id_type=pl.DeviceIdType.MESH); return 0
    lax.fori_loop(1, 16, hello, 0)
    def hello_group(r, _):
        pl.semaphore_signal(barrier, inc=1, device_id=(b, (g + r) % 8), device_id_type=pl.DeviceIdType.MESH); return 0
    lax.fori_loop(1, 8, hello_group, 0)
    pl.semaphore_wait(barrier, 22)

    def c_copy(d):
        return remote(cache_ref.at[d // 2], kvc.at[b], c_ss.at[d], c_rs.at[b], (d, g))
    def n_copy(d):
        return remote(kvnew.at[d // 2], kvn.at[b], n_ss.at[d], n_rs.at[b], (d, g))
    def q_copy(d):
        return remote(qsend.at[d], qrecv.at[b], q_ss.at[d], q_rs.at[b], (d, g))
    def d_copy(e):
        return remote(kvnew.at[e], dec_ref.at[g], d_ss.at[e], d_rs.at[g], (b, e))
    def o_copy(c):
        hi = c // 16
        return remote(osend.at[pl.ds(pl.multiple_of(c * 64, 64), 64)], orecv.at[b, pl.ds(pl.multiple_of(hi * 64, 64), 64)],
                      o_ss.at[c], o_rs.at[hi, b], (c + hi * (31 - 2 * c), g))
    def others(f):
        def body(r, _):
            f((b + r) % 16); return 0
        lax.fori_loop(1, 16, body, 0)
    def landed(buf, sem, s):
        remote(buf.at[s], buf.at[s], sem.at[s], sem.at[s], (s, g)).wait_recv()

    others(lambda d: c_copy(d).start())
    kvc[pl.ds(b, 1)] = cache_ref[pl.ds(b // 2, 1)]

    length = len_ref[0]
    j = lax.broadcasted_iota(jnp.int32, (128, 1), 0)
    pos = jnp.where(j < 64, b * 64 + j, (31 - b) * 64 + j - 64) + length
    cos, sin = rope_tables(pos.astype(F32))
    normed[...] = norm_rows(hid_ref[...], ng_ref[...])
    ones = block_ones()
    lane = lax.broadcasted_iota(jnp.int32, (128, 128), 1)
    copies[0].wait(); copies[1].wait()
    k = jnp.dot(normed[...], w[0], preferred_element_type=F32)
    v = jnp.dot(normed[...], w[1], preferred_element_type=F32)
    for t in range(4):
        kk = head_rope(k[:, t * 128:(t + 1) * 128], pair_gain(kg_ref, t), cos, sin, ones)
        vv = v[:, t * 128:(t + 1) * 128]
        kvnew[2 * t] = jnp.where(lane < 64, kk, pltpu.roll(vv, 64, 1)).astype(BF16)
        kvnew[2 * t + 1] = jnp.where(lane < 64, pltpu.roll(kk, 64, 1), vv).astype(BF16)
    others(lambda d: n_copy(d).start())
    kvn[pl.ds(b, 1)] = kvnew[pl.ds(b // 2, 1)]

    cosq, sinq = cos * QSCALE, sin * QSCALE
    for c in range(4):
        copies[2 + c].wait()
        q = jnp.dot(normed[...], w[2 + c], preferred_element_type=F32)
        for t in range(4):
            d = plane[c] * 4 + t
            gain = jnp.concatenate([qg_ref[pl.ds(2 * d, 1), :], qg_ref[pl.ds(2 * d + 1, 1), :]], 1)
            qsend[d] = head_rope(q[:, t * 128:(t + 1) * 128], gain, cosq, sinq, ones).astype(BF16)
        def send_q(t, _):
            d = plane[c] * 4 + t
            @pl.when(d != b)
            def _():
                q_copy(d).start()
            return 0
        lax.fori_loop(0, 4, send_q, 0)
    qrecv[pl.ds(b, 1)] = qsend[pl.ds(b, 1)]
    wcopies = [pltpu.make_async_copy(wo_hbm.at[:, pl.ds(512 * n, 512)], wo.at[n], wosem.at[n]) for n in range(4)]
    for cp in wcopies:
        cp.start()
    def send_dec(r, _):
        d_copy((g + r) % 8).start(); return 0
    lax.fori_loop(1, 8, send_dec, 0)
    dec_ref[pl.ds(g, 1)] = kvnew[pl.ds(g, 1)]

    def cache_block(s):
        prep_keys(kvc[s], pl.multiple_of(s * 128, 128), 128, length, kt, vo)
    cache_block(b)
    def cache_in(s):
        landed(kvc, c_rs, s)
        cache_block(s)
    others(cache_in)
    others(lambda s: landed(kvn, n_rs, s))
    def new_pair(i, _):
        lo = jnp.concatenate([kvn[2 * i, 0:64], kvn[2 * i + 1, 0:64]], 0)
        hi = jnp.concatenate([kvn[2 * i + 1, 64:128], kvn[2 * i, 64:128]], 0)
        prep_keys(lo, pl.multiple_of(2048 + i * 128, 128), 128, None, kt, vo)
        prep_keys(hi, pl.multiple_of(2048 + (15 - i) * 128, 128), 128, None, kt, vo)
        return 0
    lax.fori_loop(0, 8, new_pair, 0)
    others(lambda s: landed(qrecv, q_rs, s))
    def quad(i, _):
        prep_q(jnp.concatenate([qrecv[4 * i + n, 0:64] for n in range(4)], 0), qs, i)
        prep_q(jnp.concatenate([qrecv[4 * i + 3 - n, 64:128] for n in range(4)], 0), qs, 7 - i)
        return 0
    lax.fori_loop(0, 4, quad, 0)

    def emit(i, val):
        osend[pl.ds(pl.multiple_of(i * 256, 256), 256), :] = val
        def one(n, _):
            c = 4 * i + n
            hi = c // 16
            dest = c + hi * (31 - 2 * c)
            @pl.when(dest != b)
            def _():
                o_copy(c).start()
            @pl.when(dest == b)
            def _():
                orecv[b, pl.ds(pl.multiple_of(hi * 64, 64), 64), :] = osend[pl.ds(pl.multiple_of(c * 64, 64), 64), :]
            return 0
        lax.fori_loop(0, 4, one, 0)
    attend(qs, kt, vo, s0, s1, mx0, mx1, acc, emit)

    def o_in(s):
        for hi in range(2):
            half = orecv.at[s, pl.ds(hi * 64, 64)]
            remote(half, half, o_ss.at[s], o_rs.at[hi, s], (s, g)).wait_recv()
    others(o_in)
    for s in range(16):
        oall[:, s * 128:(s + 1) * 128] = orecv[s]
    for n in range(4):
        wcopies[n].wait()
        out_ref[:, n * 512:(n + 1) * 512] = jnp.dot(oall[...], wo[n], preferred_element_type=F32).astype(BF16)

    def drain(d):
        c_copy(d).wait_send(); n_copy(d).wait_send(); q_copy(d).wait_send()
        o_copy(d).wait_send(); o_copy(31 - d).wait_send()
    others(drain)
    def drain_dec(r, _):
        e = (g + r) % 8
        d_copy(e).wait_send()
        remote(dec_ref.at[e], dec_ref.at[e], d_ss.at[e], d_rs.at[e], (b, e)).wait_recv()
        return 0
    lax.fori_loop(1, 8, drain_dec, 0)

def shards(hidden, cache_len, cache_kv, norm_gain, w_query, w_key, w_value, q_gain, k_gain, w_out):
    vm = pl.BlockSpec(memory_space=pltpu.VMEM); hb = pl.BlockSpec(memory_space=pl.ANY)
    blocks = lambda n: pltpu.VMEM((n, 128, 128), BF16)
    dma = pltpu.SemaphoreType.DMA
    out, dec = pl.pallas_call(layer_kernel,
        out_shape=(jax.ShapeDtypeStruct((128, 2048), BF16), jax.ShapeDtypeStruct((8, 128, 128), BF16)),
        in_specs=[pl.BlockSpec(memory_space=pltpu.SMEM), vm, vm, vm, vm, vm, hb, hb, hb, hb], out_specs=(vm, vm),
        scratch_shapes=[pltpu.VMEM((6, 2048, 512), BF16), pltpu.VMEM((4, 2048, 512), BF16), pltpu.VMEM((128, 2048), BF16),
            blocks(8), blocks(16), blocks(16), blocks(16), blocks(16), pltpu.VMEM((2048, 128), BF16), blocks(16),
            pltpu.VMEM((128, 2048), BF16), pltpu.VMEM((8, 512, 128), BF16), pltpu.VMEM((128, 4096), BF16),
            pltpu.VMEM((4096, 128), BF16), pltpu.VMEM((512, 4096), F32), pltpu.VMEM((512, 4096), F32),
            pltpu.VMEM((512, 128), F32), pltpu.VMEM((512, 128), F32), pltpu.VMEM((512, 128), F32),
            dma((6,)), dma((4,))] + [dma((16,))] * 6 + [dma((8,))] * 2 + [dma((32,)), dma((2, 16))],
        compiler_params=pltpu.CompilerParams(vmem_limit_bytes=60 << 20, collective_id=0, has_side_effects=True),
        name="layer")(cache_len, hidden[0], cache_kv[0].transpose(1, 0, 2), norm_gain[None], q_gain, k_gain,
                      w_key, w_value, w_query, w_out)
    return out[None], dec[:, :, None, :]


def solution(mesh):
    from jax.sharding import PartitionSpec as P
    in_specs = (P("group", "blk", None), P("group"), P("group", "blk", None, None)) + (P(),) * 7
    out_specs = (P("group", "blk", None), P(None, "blk", "group", None))
    return jax.shard_map(shards, mesh=mesh, in_specs=in_specs, out_specs=out_specs, check_vma=False)
```

```python
import functools, math
import jax, jax.numpy as jnp
from jax import lax
from jax.experimental import pallas as pl
from jax.experimental.pallas import tpu as pltpu
F32, BF16 = jnp.float32, jnp.bfloat16
NEG = -1e30

def prep_keys(src, row0, rows, length, kt_ref, vo_ref):
    x = src.astype(F32)
    lane = lax.broadcasted_iota(jnp.int32, x.shape, 1)
    if length is None:
        bias = jnp.zeros_like(x)
    else:
        row = lax.broadcasted_iota(jnp.int32, x.shape, 0) + row0
        bias = jnp.where(row < length, 0.0, NEG)
    k = jnp.where(lane < 64, x, bias)
    kt_ref[:, pl.ds(row0, rows)] = k.T.astype(BF16)
    vo_ref[pl.ds(row0, rows), :] = jnp.where(lane < 64, 1.0, x).astype(BF16)

def prep_q(src, qs_ref, i):
    x = src.astype(F32)
    lane = lax.broadcasted_iota(jnp.int32, x.shape, 1)
    tail = jnp.where(lane == 64, 1.0, 0.0)
    qs_ref[i, 0:256, :] = jnp.where(lane < 64, x, tail).astype(BF16)
    qs_ref[i, 256:512, :] = jnp.where(lane < 64, pltpu.roll(x, 64, 1), tail).astype(BF16)

KB = 512
def attend(qs, kt, vo, s0, s1, mx0, mx1, accs, ms, arrived, emit):
    n = 2048 // KB
    def qk(i, base, c, s, mx, diag=None):
        off = pl.multiple_of(c * KB, KB)
        sc = jnp.dot(qs[i], kt[:, pl.ds(pl.multiple_of(base + off, KB), KB)], preferred_element_type=F32)
        if diag is not None:
            r = lax.broadcasted_iota(jnp.int32, (512, KB), 0)
            r = jnp.where(r >= 256, r - 256, r) + diag * 256
            col = lax.broadcasted_iota(jnp.int32, (512, KB), 1)
            sc = jnp.where(col <= r, sc, NEG)
        s[:, pl.ds(off, KB)] = sc
        mm = sc[:, 0:128]
        for l in range(1, KB // 128):
            mm = jnp.maximum(mm, sc[:, l * 128:(l + 1) * 128])
        mx[...] = jnp.maximum(mx[...], mm)
    def pv(base, c, s, mx):
        off = pl.multiple_of(c * KB, KB)
        m = mx[...]
        p = jnp.exp2(s[:, pl.ds(off, KB)] - jnp.concatenate([m] * (KB // 128), 1)).astype(BF16)
        return jnp.dot(p, vo[pl.ds(pl.multiple_of(base + off, KB), KB), :], preferred_element_type=F32)
    def row_max(mx):
        return jnp.broadcast_to(jnp.max(mx[...], 1, keepdims=True), mx.shape)

    def cached(inext, i, s, mx, t, tmx):
        if inext is not None:
            tmx[...] = jnp.full(tmx.shape, NEG, F32)
        tot = None
        for c in range(n):
            if inext is not None:
                qk(inext, 0, c, t, tmx)
            part = pv(0, c, s, mx)
            tot = part if tot is None else tot + part
        accs[i] = tot
        if inext is not None:
            m = row_max(tmx)
            tmx[...] = m
            ms[inext] = m
    mx0[...] = jnp.full(mx0.shape, NEG, F32)
    for c in range(n):
        qk(0, 0, c, s0, mx0)
    m = row_max(mx0)
    mx0[...] = m
    ms[0] = m
    def cached_pair(t, _):
        cached(2 * t + 1, 2 * t, s0, mx0, s1, mx1)
        cached(2 * t + 2, 2 * t + 1, s1, mx1, s0, mx0)
        return 0
    lax.fori_loop(0, 3, cached_pair, 0)
    cached(7, 6, s0, mx0, s1, mx1)
    cached(None, 7, s1, mx1, None, None)

    arrived()
    def start(i, mx):
        mx[...] = ms[i]
    def finish_max(i, mx):
        m = row_max(mx)
        mx[...] = m
        accs[i] = accs[i] * jnp.exp2(ms[i] - m)
    def out(i):
        a = accs[i]
        lane = lax.broadcasted_iota(jnp.int32, (256, 128), 1)
        h0, h1 = a[0:256], a[256:512]
        num = jnp.where(lane < 64, pltpu.roll(h0, 64, 1), h1)
        den = jnp.where(lane < 64, h0, pltpu.roll(h1, 64, 1))
        emit(i, (num / den).astype(BF16))
    def add(i, c, s, mx):
        accs[i] += pv(2048, c, s, mx)
    start(0, mx0)
    qk(0, 2048, 0, s0, mx0, diag=0)
    finish_max(0, mx0)
    def odd(t):
        i = 2 * t
        start(i + 1, mx1)
        def a(c, _):
            qk(i + 1, 2048, c, s1, mx1); add(i, c, s0, mx0); return 0
        lax.fori_loop(0, t, a, 0)
        qk(i + 1, 2048, t, s1, mx1, diag=1); add(i, t, s0, mx0)
        finish_max(i + 1, mx1); out(i)
    def pair(t, _):
        odd(t)
        i = 2 * t + 1
        start(i + 1, mx0)
        def a(c, _):
            qk(i + 1, 2048, c, s0, mx0); add(i, c, s1, mx1); return 0
        lax.fori_loop(0, t + 1, a, 0)
        qk(i + 1, 2048, t + 1, s0, mx0, diag=0)
        finish_max(i + 1, mx0); out(i)
        return 0
    lax.fori_loop(0, 3, pair, 0)
    odd(3)
    tot = accs[7]
    for c in range(n):
        tot = tot + pv(2048, c, s1, mx1)
    accs[7] = tot
    out(7)

EPS=1e-5; THETA=1e6
QSCALE = 0.125 * math.log2(math.e)

def rope_tables(pos_f):
    lane = lax.broadcasted_iota(jnp.int32, (1, 128), 1)
    inv = jnp.exp(lax.rem(lane, 32).astype(F32) * (-2.0 / 64.0 * math.log(THETA)))
    ang = pos_f * inv
    sgn = jnp.where(lax.rem(lane, 64) < 32, -1.0, 1.0)
    return jnp.cos(ang), jnp.sin(ang) * sgn

def norm_rows(hid, gain):
    x = hid.astype(F32)
    return (x * lax.rsqrt(jnp.mean(x * x, -1, keepdims=True) + EPS) * gain).astype(BF16)

def block_ones():
    a = lax.broadcasted_iota(jnp.int32, (128, 128), 0) // 64
    b = lax.broadcasted_iota(jnp.int32, (128, 128), 1) // 64
    return jnp.where(a == b, 1.0, 0.0).astype(BF16)

def head_rope(x, gain, cos, sin, ones):
    sq = x * x
    hi = sq.astype(BF16)
    lo = (sq - hi.astype(F32)).astype(BF16)
    tot = jnp.dot(hi, ones, preferred_element_type=F32) + jnp.dot(lo, ones, preferred_element_type=F32)
    n = x * lax.rsqrt(tot * (1.0 / 64) + EPS) * gain
    lane = lax.broadcasted_iota(jnp.int32, n.shape, 1)
    sw = jnp.where(lax.rem(lane, 64) < 32, pltpu.roll(n, 96, 1), pltpu.roll(n, 32, 1))
    return n * cos + sw * sin

def pair_gain(g_ref, j):
    return jnp.concatenate([g_ref[2 * j:2 * j + 1, :], g_ref[2 * j + 1:2 * j + 2, :]], 1)

def remote(src, dst, ssem, rsem, dev):
    return pltpu.make_async_remote_copy(src_ref=src, dst_ref=dst, send_sem=ssem, recv_sem=rsem,
                                        device_id=dev, device_id_type=pl.DeviceIdType.MESH)

def layer_kernel(len_ref, hid_ref, cache_ref, ng_ref, qg_ref, kg_ref, wk_hbm, wv_hbm, wq_hbm, wo_hbm, out_ref, dec_ref,
                 w, wo, normed, kvnew, qsend, kvc, kvn, qrecv, osend, orecv, oall, qs, kt, vo, s0, s1, mx0, mx1, accs, ms, heads,
                 wsem, wosem, c_ss, c_rs, n_ss, n_rs, q_ss, q_rs, d_ss, d_rs, o_ss, o_rs):
    b = lax.axis_index("blk"); g = lax.axis_index("group")
    def col(n):
        return pl.ds(pl.multiple_of(n * 512, 512), 512)
    plane = [(b // 4 + 1 + c) % 4 for c in range(4)]
    copies = [pltpu.make_async_copy(wq_hbm.at[:, col(plane[c])], w.at[c], wsem.at[c]) for c in range(4)]
    copies += [pltpu.make_async_copy(wk_hbm, w.at[4], wsem.at[4]), pltpu.make_async_copy(wv_hbm, w.at[5], wsem.at[5])]
    for cp in copies:
        cp.start()
    barrier = pltpu.get_barrier_semaphore()
    def hello(r, _):
        pl.semaphore_signal(barrier, inc=1, device_id=((b + r) % 16, g), device_id_type=pl.DeviceIdType.MESH); return 0
    lax.fori_loop(1, 16, hello, 0)
    def hello_group(r, _):
        pl.semaphore_signal(barrier, inc=1, device_id=(b, (g + r) % 8), device_id_type=pl.DeviceIdType.MESH); return 0
    lax.fori_loop(1, 8, hello_group, 0)
    heads[...] = jnp.swapaxes(cache_ref[...].astype(F32), 0, 1).astype(BF16)
    pl.semaphore_wait(barrier, 22)

    def c_copy(d):
        return remote(heads.at[d // 2], kvc.at[b], c_ss.at[d], c_rs.at[b], (d, g))
    def n_copy(d):
        return remote(kvnew.at[d // 2], kvn.at[b], n_ss.at[d], n_rs.at[b], (d, g))
    def q_copy(d):
        return remote(qsend.at[d], qrecv.at[b], q_ss.at[d], q_rs.at[b], (d, g))
    def d_copy(e):
        return remote(kvnew.at[e], dec_ref.at[g], d_ss.at[e], d_rs.at[g], (b, e))
    def o_copy(c):
        hi = c // 16
        return remote(osend.at[pl.ds(pl.multiple_of(c * 64, 64), 64)], orecv.at[b, pl.ds(pl.multiple_of(hi * 64, 64), 64)],
                      o_ss.at[c], o_rs.at[hi, b], (c + hi * (31 - 2 * c), g))
    def others(f):
        def body(r, _):
            f((b + r) % 16); return 0
        lax.fori_loop(1, 16, body, 0)
    def landed(buf, sem, s):
        remote(buf.at[s], buf.at[s], sem.at[s], sem.at[s], (s, g)).wait_recv()

    others(lambda d: c_copy(d).start())
    kvc[pl.ds(b, 1)] = heads[pl.ds(b // 2, 1)]

    length = len_ref[0]
    j = lax.broadcasted_iota(jnp.int32, (128, 1), 0)
    pos = jnp.where(j < 64, b * 64 + j, (31 - b) * 64 + j - 64) + length
    cos, sin = rope_tables(pos.astype(F32))
    normed[...] = norm_rows(hid_ref[...], ng_ref[...])
    ones = block_ones()
    lane = lax.broadcasted_iota(jnp.int32, (128, 128), 1)
    cosq, sinq = cos * QSCALE, sin * QSCALE
    for c in range(4):
        copies[c].wait()
        q = jnp.dot(normed[...], w[c], preferred_element_type=F32)
        for t in range(4):
            d = plane[c] * 4 + t
            gain = jnp.concatenate([qg_ref[pl.ds(2 * d, 1), :], qg_ref[pl.ds(2 * d + 1, 1), :]], 1)
            qsend[d] = head_rope(q[:, t * 128:(t + 1) * 128], gain, cosq, sinq, ones).astype(BF16)
        def send_q(t, _):
            d = plane[c] * 4 + t
            @pl.when(d != b)
            def _():
                q_copy(d).start()
            return 0
        lax.fori_loop(0, 4, send_q, 0)
    qrecv[pl.ds(b, 1)] = qsend[pl.ds(b, 1)]
    copies[4].wait(); copies[5].wait()
    k = jnp.dot(normed[...], w[4], preferred_element_type=F32)
    v = jnp.dot(normed[...], w[5], preferred_element_type=F32)
    for t in range(4):
        kk = head_rope(k[:, t * 128:(t + 1) * 128], pair_gain(kg_ref, t), cos, sin, ones)
        vv = v[:, t * 128:(t + 1) * 128]
        kvnew[2 * t] = jnp.where(lane < 64, kk, pltpu.roll(vv, 64, 1)).astype(BF16)
        kvnew[2 * t + 1] = jnp.where(lane < 64, pltpu.roll(kk, 64, 1), vv).astype(BF16)
    others(lambda d: n_copy(d).start())
    kvn[pl.ds(b, 1)] = kvnew[pl.ds(b // 2, 1)]

    wcopies = [pltpu.make_async_copy(wo_hbm.at[:, pl.ds(512 * n, 512)], wo.at[n], wosem.at[n]) for n in range(4)]
    for cp in wcopies:
        cp.start()
    def send_dec(r, _):
        d_copy((g + r) % 8).start(); return 0
    lax.fori_loop(1, 8, send_dec, 0)
    dec_ref[pl.ds(g, 1)] = kvnew[pl.ds(g, 1)]

    def cache_block(s):
        prep_keys(kvc[s], pl.multiple_of(s * 128, 128), 128, length, kt, vo)
    cache_block(b)
    def cache_in(s):
        landed(kvc, c_rs, s)
        cache_block(s)
    others(cache_in)
    others(lambda s: landed(qrecv, q_rs, s))
    def quad(i, _):
        prep_q(jnp.concatenate([qrecv[4 * i + n, 0:64] for n in range(4)], 0), qs, i)
        prep_q(jnp.concatenate([qrecv[4 * i + 3 - n, 64:128] for n in range(4)], 0), qs, 7 - i)
        return 0
    lax.fori_loop(0, 4, quad, 0)
    def arrived():
        others(lambda s: landed(kvn, n_rs, s))
        def new_pair(i, _):
            lo = jnp.concatenate([kvn[2 * i, 0:64], kvn[2 * i + 1, 0:64]], 0)
            hi = jnp.concatenate([kvn[2 * i + 1, 64:128], kvn[2 * i, 64:128]], 0)
            prep_keys(lo, pl.multiple_of(2048 + i * 128, 128), 128, None, kt, vo)
            prep_keys(hi, pl.multiple_of(2048 + (15 - i) * 128, 128), 128, None, kt, vo)
            return 0
        lax.fori_loop(0, 8, new_pair, 0)
    def emit(i, val):
        osend[pl.ds(pl.multiple_of(i * 256, 256), 256), :] = val
        def one(n, _):
            c = 4 * i + n
            hi = c // 16
            dest = c + hi * (31 - 2 * c)
            @pl.when(dest != b)
            def _():
                o_copy(c).start()
            @pl.when(dest == b)
            def _():
                orecv[b, pl.ds(pl.multiple_of(hi * 64, 64), 64), :] = osend[pl.ds(pl.multiple_of(c * 64, 64), 64), :]
            return 0
        lax.fori_loop(0, 4, one, 0)
    attend(qs, kt, vo, s0, s1, mx0, mx1, accs, ms, arrived, emit)

    def o_in(s):
        for hi in range(2):
            half = orecv.at[s, pl.ds(hi * 64, 64)]
            remote(half, half, o_ss.at[s], o_rs.at[hi, s], (s, g)).wait_recv()
    others(o_in)
    for s in range(16):
        oall[:, s * 128:(s + 1) * 128] = orecv[s]
    for n in range(4):
        wcopies[n].wait()
        out_ref[:, n * 512:(n + 1) * 512] = jnp.dot(oall[...], wo[n], preferred_element_type=F32).astype(BF16)

    def drain(d):
        c_copy(d).wait_send(); n_copy(d).wait_send(); q_copy(d).wait_send()
        o_copy(d).wait_send(); o_copy(31 - d).wait_send()
    others(drain)
    def drain_dec(r, _):
        e = (g + r) % 8
        d_copy(e).wait_send()
        remote(dec_ref.at[e], dec_ref.at[e], d_ss.at[e], d_rs.at[e], (b, e)).wait_recv()
        return 0
    lax.fori_loop(1, 8, drain_dec, 0)

def shards(hidden, cache_len, cache_kv, norm_gain, w_query, w_key, w_value, q_gain, k_gain, w_out):
    vm = pl.BlockSpec(memory_space=pltpu.VMEM); hb = pl.BlockSpec(memory_space=pl.ANY)
    blocks = lambda n: pltpu.VMEM((n, 128, 128), BF16)
    dma = pltpu.SemaphoreType.DMA
    out, dec = pl.pallas_call(layer_kernel,
        out_shape=(jax.ShapeDtypeStruct((128, 2048), BF16), jax.ShapeDtypeStruct((8, 128, 128), BF16)),
        in_specs=[pl.BlockSpec(memory_space=pltpu.SMEM), vm, vm, vm, vm, vm, hb, hb, hb, hb], out_specs=(vm, vm),
        scratch_shapes=[pltpu.VMEM((6, 2048, 512), BF16), pltpu.VMEM((4, 2048, 512), BF16), pltpu.VMEM((128, 2048), BF16),
            blocks(8), blocks(16), blocks(16), blocks(16), blocks(16), pltpu.VMEM((2048, 128), BF16), blocks(16),
            pltpu.VMEM((128, 2048), BF16), pltpu.VMEM((8, 512, 128), BF16), pltpu.VMEM((128, 4096), BF16),
            pltpu.VMEM((4096, 128), BF16), pltpu.VMEM((512, 2048), F32), pltpu.VMEM((512, 2048), F32),
            pltpu.VMEM((512, 128), F32), pltpu.VMEM((512, 128), F32), pltpu.VMEM((8, 512, 128), F32), pltpu.VMEM((8, 512, 128), F32), blocks(8),
            dma((6,)), dma((4,))] + [dma((16,))] * 6 + [dma((8,))] * 2 + [dma((32,)), dma((2, 16))],
        compiler_params=pltpu.CompilerParams(vmem_limit_bytes=54 << 20, collective_id=0, has_side_effects=True),
        name="layer")(cache_len, hidden[0], cache_kv[0], norm_gain[None], q_gain, k_gain,
                      w_key, w_value, w_query, w_out)
    return out[None], dec[:, :, None, :]


def solution(mesh):
    from jax.sharding import PartitionSpec as P
    in_specs = (P("group", "blk", None), P("group"), P("group", "blk", None, None)) + (P(),) * 7
    out_specs = (P("group", "blk", None), P(None, "blk", "group", None))
    return jax.shard_map(shards, mesh=mesh, in_specs=in_specs, out_specs=out_specs, check_vma=False)
```

```python
import functools, math
import jax, jax.numpy as jnp
from jax import lax
from jax.experimental import pallas as pl
from jax.experimental.pallas import tpu as pltpu
F32, BF16 = jnp.float32, jnp.bfloat16
NEG = -1e30

def prep_keys(src, row0, rows, length, kt_ref, vo_ref):
    x = src.astype(F32)
    lane = lax.broadcasted_iota(jnp.int32, x.shape, 1)
    if length is None:
        bias = jnp.zeros_like(x)
    else:
        row = lax.broadcasted_iota(jnp.int32, x.shape, 0) + row0
        bias = jnp.where(row < length, 0.0, NEG)
    k = jnp.where(lane < 64, x, bias)
    kt_ref[:, pl.ds(row0, rows)] = k.T.astype(BF16)
    vo_ref[pl.ds(row0, rows), :] = jnp.where(lane < 64, 1.0, x).astype(BF16)

def prep_q(src, qs_ref, i):
    x = src.astype(F32)
    lane = lax.broadcasted_iota(jnp.int32, x.shape, 1)
    tail = jnp.where(lane == 64, 1.0, 0.0)
    qs_ref[i, 0:256, :] = jnp.where(lane < 64, x, tail).astype(BF16)
    qs_ref[i, 256:512, :] = jnp.where(lane < 64, pltpu.roll(x, 64, 1), tail).astype(BF16)

KB = 512
def attend(qs, kt, vo, s0, s1, mx0, mx1, accs, ms, arrived, emit):
    n = 2048 // KB
    def qk(i, base, c, s, mx, diag=None, width=KB):
        off = c * KB
        sc = jnp.dot(qs[i], kt[:, base + off:base + off + width], preferred_element_type=F32)
        if diag is not None:
            r = lax.broadcasted_iota(jnp.int32, (512, width), 0)
            r = jnp.where(r >= 256, r - 256, r) + diag * 256
            col = lax.broadcasted_iota(jnp.int32, (512, width), 1)
            sc = jnp.where(col <= r, sc, NEG)
        s[:, off:off + width] = sc
        mm = sc[:, 0:128]
        for l in range(1, width // 128):
            mm = jnp.maximum(mm, sc[:, l * 128:(l + 1) * 128])
        mx[...] = jnp.maximum(mx[...], mm)
    def pv(base, c, s, mx, width=KB):
        off = c * KB
        m = mx[...]
        p = jnp.exp2(s[:, off:off + width] - jnp.concatenate([m] * (width // 128), 1)).astype(BF16)
        return jnp.dot(p, vo[base + off:base + off + width, :], preferred_element_type=F32)
    def row_max(mx):
        return jnp.broadcast_to(jnp.max(mx[...], 1, keepdims=True), mx.shape)

    def cached(inext, i, s, mx, t, tmx):
        if inext is not None:
            tmx[...] = jnp.full(tmx.shape, NEG, F32)
        tot = None
        for c in range(n):
            if inext is not None:
                qk(inext, 0, c, t, tmx)
            part = pv(0, c, s, mx)
            tot = part if tot is None else tot + part
        accs[i] = tot
        if inext is not None:
            m = row_max(tmx)
            tmx[...] = m
            ms[inext] = m
    mx0[...] = jnp.full(mx0.shape, NEG, F32)
    for c in range(n):
        qk(0, 0, c, s0, mx0)
    m = row_max(mx0)
    mx0[...] = m
    ms[0] = m
    def cached_pair(t, _):
        cached(2 * t + 1, 2 * t, s0, mx0, s1, mx1)
        cached(2 * t + 2, 2 * t + 1, s1, mx1, s0, mx0)
        return 0
    lax.fori_loop(0, 3, cached_pair, 0)
    cached(7, 6, s0, mx0, s1, mx1)
    cached(None, 7, s1, mx1, None, None)

    arrived()
    def start(i, mx):
        mx[...] = ms[i]
    def finish_max(i, mx):
        m = row_max(mx)
        mx[...] = m
        accs[i] = accs[i] * jnp.exp2(ms[i] - m)
    def out(i):
        a = accs[i]
        lane = lax.broadcasted_iota(jnp.int32, (256, 128), 1)
        h0, h1 = a[0:256], a[256:512]
        num = jnp.where(lane < 64, pltpu.roll(h0, 64, 1), h1)
        den = jnp.where(lane < 64, h0, pltpu.roll(h1, 64, 1))
        emit(i, (num / den).astype(BF16))
    def width(i, c):
        return 256 if i % 2 == 0 and c == i // 2 else KB
    def scores(i, c, s, mx):
        qk(i, 2048, c, s, mx, i % 2 if c == i // 2 else None, width(i, c))
    bufs = [(s0, mx0), (s1, mx1)]
    start(0, mx0)
    scores(0, 0, s0, mx0)
    finish_max(0, mx0)
    for i in range(8):
        s, mx = bufs[i % 2]
        t, tmx = bufs[1 - i % 2]
        if i < 7:
            start(i + 1, tmx)
        tot = accs[i]
        for c in range(min(i + 1, 7) // 2 + 1):
            if i < 7:
                scores(i + 1, c, t, tmx)
            if c <= i // 2:
                tot = tot + pv(2048, c, s, mx, width(i, c))
        accs[i] = tot
        if i < 7:
            finish_max(i + 1, tmx)
        out(i)

EPS=1e-5; THETA=1e6
QSCALE = 0.125 * math.log2(math.e)

def rope_tables(pos_f):
    lane = lax.broadcasted_iota(jnp.int32, (1, 128), 1)
    inv = jnp.exp(lax.rem(lane, 32).astype(F32) * (-2.0 / 64.0 * math.log(THETA)))
    ang = pos_f * inv
    sgn = jnp.where(lax.rem(lane, 64) < 32, -1.0, 1.0)
    return jnp.cos(ang), jnp.sin(ang) * sgn

def norm_rows(hid, gain):
    x = hid.astype(F32)
    return (x * lax.rsqrt(jnp.mean(x * x, -1, keepdims=True) + EPS) * gain).astype(BF16)

def block_ones():
    a = lax.broadcasted_iota(jnp.int32, (128, 128), 0) // 64
    b = lax.broadcasted_iota(jnp.int32, (128, 128), 1) // 64
    return jnp.where(a == b, 1.0, 0.0).astype(BF16)

def head_rope(x, gain, cos, sin, ones):
    sq = x * x
    hi = sq.astype(BF16)
    lo = (sq - hi.astype(F32)).astype(BF16)
    tot = jnp.dot(hi, ones, preferred_element_type=F32) + jnp.dot(lo, ones, preferred_element_type=F32)
    n = x * lax.rsqrt(tot * (1.0 / 64) + EPS) * gain
    lane = lax.broadcasted_iota(jnp.int32, n.shape, 1)
    sw = jnp.where(lax.rem(lane, 64) < 32, pltpu.roll(n, 96, 1), pltpu.roll(n, 32, 1))
    return n * cos + sw * sin

def pair_gain(g_ref, j):
    return jnp.concatenate([g_ref[2 * j:2 * j + 1, :], g_ref[2 * j + 1:2 * j + 2, :]], 1)

def remote(src, dst, ssem, rsem, dev):
    return pltpu.make_async_remote_copy(src_ref=src, dst_ref=dst, send_sem=ssem, recv_sem=rsem,
                                        device_id=dev, device_id_type=pl.DeviceIdType.MESH)

def layer_kernel(len_ref, hid_ref, cache_ref, ng_ref, qg_ref, kg_ref, wk_hbm, wv_hbm, wq_hbm, wo_hbm, out_ref, dec_ref,
                 w, wo, normed, kvnew, qsend, kvc, kvn, qrecv, osend, orecv, oall, qs, kt, vo, s0, s1, mx0, mx1, accs, ms, heads,
                 wsem, wosem, c_ss, c_rs, n_ss, n_rs, q_ss, q_rs, d_ss, d_rs, o_ss, o_rs):
    b = lax.axis_index("blk"); g = lax.axis_index("group")
    def col(n):
        return pl.ds(pl.multiple_of(n * 512, 512), 512)
    plane = [(b // 4 + 1 + c) % 4 for c in range(4)]
    copies = [pltpu.make_async_copy(wq_hbm.at[:, col(plane[c])], w.at[c], wsem.at[c]) for c in range(4)]
    copies += [pltpu.make_async_copy(wk_hbm, w.at[4], wsem.at[4]), pltpu.make_async_copy(wv_hbm, w.at[5], wsem.at[5])]
    for cp in copies:
        cp.start()
    barrier = pltpu.get_barrier_semaphore()
    def hello(r, _):
        pl.semaphore_signal(barrier, inc=1, device_id=((b + r) % 16, g), device_id_type=pl.DeviceIdType.MESH); return 0
    lax.fori_loop(1, 16, hello, 0)
    def hello_group(r, _):
        pl.semaphore_signal(barrier, inc=1, device_id=(b, (g + r) % 8), device_id_type=pl.DeviceIdType.MESH); return 0
    lax.fori_loop(1, 8, hello_group, 0)
    heads[...] = jnp.swapaxes(cache_ref[...].astype(F32), 0, 1).astype(BF16)
    pl.semaphore_wait(barrier, 22)

    def c_copy(d):
        return remote(heads.at[d // 2], kvc.at[b], c_ss.at[d], c_rs.at[b], (d, g))
    def n_copy(d):
        return remote(kvnew.at[d // 2], kvn.at[b], n_ss.at[d], n_rs.at[b], (d, g))
    def q_copy(d):
        return remote(qsend.at[d], qrecv.at[b], q_ss.at[d], q_rs.at[b], (d, g))
    def d_copy(e):
        return remote(kvnew.at[e], dec_ref.at[g], d_ss.at[e], d_rs.at[g], (b, e))
    def o_copy(c):
        hi = c // 16
        return remote(osend.at[pl.ds(pl.multiple_of(c * 64, 64), 64)], orecv.at[b, pl.ds(pl.multiple_of(hi * 64, 64), 64)],
                      o_ss.at[c], o_rs.at[hi, b], (c + hi * (31 - 2 * c), g))
    def others(f):
        def body(r, _):
            f((b + r) % 16); return 0
        lax.fori_loop(1, 16, body, 0)
    def landed(buf, sem, s):
        remote(buf.at[s], buf.at[s], sem.at[s], sem.at[s], (s, g)).wait_recv()

    others(lambda d: c_copy(d).start())
    kvc[pl.ds(b, 1)] = heads[pl.ds(b // 2, 1)]

    length = len_ref[0]
    j = lax.broadcasted_iota(jnp.int32, (128, 1), 0)
    pos = jnp.where(j < 64, b * 64 + j, (31 - b) * 64 + j - 64) + length
    cos, sin = rope_tables(pos.astype(F32))
    normed[...] = norm_rows(hid_ref[...], ng_ref[...])
    ones = block_ones()
    lane = lax.broadcasted_iota(jnp.int32, (128, 128), 1)
    cosq, sinq = cos * QSCALE, sin * QSCALE
    for c in range(4):
        copies[c].wait()
        q = jnp.dot(normed[...], w[c], preferred_element_type=F32)
        for t in range(4):
            d = plane[c] * 4 + t
            gain = jnp.concatenate([qg_ref[pl.ds(2 * d, 1), :], qg_ref[pl.ds(2 * d + 1, 1), :]], 1)
            qsend[d] = head_rope(q[:, t * 128:(t + 1) * 128], gain, cosq, sinq, ones).astype(BF16)
        def send_q(t, _):
            d = plane[c] * 4 + t
            @pl.when(d != b)
            def _():
                q_copy(d).start()
            return 0
        lax.fori_loop(0, 4, send_q, 0)
    qrecv[pl.ds(b, 1)] = qsend[pl.ds(b, 1)]
    copies[4].wait(); copies[5].wait()
    k = jnp.dot(normed[...], w[4], preferred_element_type=F32)
    v = jnp.dot(normed[...], w[5], preferred_element_type=F32)
    for t in range(4):
        kk = head_rope(k[:, t * 128:(t + 1) * 128], pair_gain(kg_ref, t), cos, sin, ones)
        vv = v[:, t * 128:(t + 1) * 128]
        kvnew[2 * t] = jnp.where(lane < 64, kk, pltpu.roll(vv, 64, 1)).astype(BF16)
        kvnew[2 * t + 1] = jnp.where(lane < 64, pltpu.roll(kk, 64, 1), vv).astype(BF16)
    others(lambda d: n_copy(d).start())
    kvn[pl.ds(b, 1)] = kvnew[pl.ds(b // 2, 1)]

    wcopies = [pltpu.make_async_copy(wo_hbm.at[:, pl.ds(512 * n, 512)], wo.at[n], wosem.at[n]) for n in range(4)]
    for cp in wcopies:
        cp.start()
    def send_dec(r, _):
        d_copy((g + r) % 8).start(); return 0
    lax.fori_loop(1, 8, send_dec, 0)
    dec_ref[pl.ds(g, 1)] = kvnew[pl.ds(g, 1)]

    def cache_block(s):
        prep_keys(kvc[s], pl.multiple_of(s * 128, 128), 128, length, kt, vo)
    cache_block(b)
    def cache_in(s):
        landed(kvc, c_rs, s)
        cache_block(s)
    others(cache_in)
    others(lambda s: landed(qrecv, q_rs, s))
    def quad(i, _):
        prep_q(jnp.concatenate([qrecv[4 * i + n, 0:64] for n in range(4)], 0), qs, i)
        prep_q(jnp.concatenate([qrecv[4 * i + 3 - n, 64:128] for n in range(4)], 0), qs, 7 - i)
        return 0
    lax.fori_loop(0, 4, quad, 0)
    def arrived():
        others(lambda s: landed(kvn, n_rs, s))
        def new_pair(i, _):
            lo = jnp.concatenate([kvn[2 * i, 0:64], kvn[2 * i + 1, 0:64]], 0)
            hi = jnp.concatenate([kvn[2 * i + 1, 64:128], kvn[2 * i, 64:128]], 0)
            prep_keys(lo, pl.multiple_of(2048 + i * 128, 128), 128, None, kt, vo)
            prep_keys(hi, pl.multiple_of(2048 + (15 - i) * 128, 128), 128, None, kt, vo)
            return 0
        lax.fori_loop(0, 8, new_pair, 0)
    def emit(i, val):
        osend[pl.ds(pl.multiple_of(i * 256, 256), 256), :] = val
        def one(n, _):
            c = 4 * i + n
            hi = c // 16
            dest = c + hi * (31 - 2 * c)
            @pl.when(dest != b)
            def _():
                o_copy(c).start()
            @pl.when(dest == b)
            def _():
                orecv[b, pl.ds(pl.multiple_of(hi * 64, 64), 64), :] = osend[pl.ds(pl.multiple_of(c * 64, 64), 64), :]
            return 0
        lax.fori_loop(0, 4, one, 0)
    attend(qs, kt, vo, s0, s1, mx0, mx1, accs, ms, arrived, emit)

    def o_in(s):
        for hi in range(2):
            half = orecv.at[s, pl.ds(hi * 64, 64)]
            remote(half, half, o_ss.at[s], o_rs.at[hi, s], (s, g)).wait_recv()
    others(o_in)
    for s in range(16):
        oall[:, s * 128:(s + 1) * 128] = orecv[s]
    for n in range(4):
        wcopies[n].wait()
        out_ref[:, n * 512:(n + 1) * 512] = jnp.dot(oall[...], wo[n], preferred_element_type=F32).astype(BF16)

    def drain(d):
        c_copy(d).wait_send(); n_copy(d).wait_send(); q_copy(d).wait_send()
        o_copy(d).wait_send(); o_copy(31 - d).wait_send()
    others(drain)
    def drain_dec(r, _):
        e = (g + r) % 8
        d_copy(e).wait_send()
        remote(dec_ref.at[e], dec_ref.at[e], d_ss.at[e], d_rs.at[e], (b, e)).wait_recv()
        return 0
    lax.fori_loop(1, 8, drain_dec, 0)

def shards(hidden, cache_len, cache_kv, norm_gain, w_query, w_key, w_value, q_gain, k_gain, w_out):
    vm = pl.BlockSpec(memory_space=pltpu.VMEM); hb = pl.BlockSpec(memory_space=pl.ANY)
    blocks = lambda n: pltpu.VMEM((n, 128, 128), BF16)
    dma = pltpu.SemaphoreType.DMA
    out, dec = pl.pallas_call(layer_kernel,
        out_shape=(jax.ShapeDtypeStruct((128, 2048), BF16), jax.ShapeDtypeStruct((8, 128, 128), BF16)),
        in_specs=[pl.BlockSpec(memory_space=pltpu.SMEM), vm, vm, vm, vm, vm, hb, hb, hb, hb], out_specs=(vm, vm),
        scratch_shapes=[pltpu.VMEM((6, 2048, 512), BF16), pltpu.VMEM((4, 2048, 512), BF16), pltpu.VMEM((128, 2048), BF16),
            blocks(8), blocks(16), blocks(16), blocks(16), blocks(16), pltpu.VMEM((2048, 128), BF16), blocks(16),
            pltpu.VMEM((128, 2048), BF16), pltpu.VMEM((8, 512, 128), BF16), pltpu.VMEM((128, 4096), BF16),
            pltpu.VMEM((4096, 128), BF16), pltpu.VMEM((512, 2048), F32), pltpu.VMEM((512, 2048), F32),
            pltpu.VMEM((512, 128), F32), pltpu.VMEM((512, 128), F32), pltpu.VMEM((8, 512, 128), F32), pltpu.VMEM((8, 512, 128), F32), blocks(8),
            dma((6,)), dma((4,))] + [dma((16,))] * 6 + [dma((8,))] * 2 + [dma((32,)), dma((2, 16))],
        compiler_params=pltpu.CompilerParams(vmem_limit_bytes=52 << 20, collective_id=0, has_side_effects=True),
        name="layer")(cache_len, hidden[0], cache_kv[0], norm_gain[None], q_gain, k_gain,
                      w_key, w_value, w_query, w_out)
    return out[None], dec[:, :, None, :]


def solution(mesh):
    from jax.sharding import PartitionSpec as P
    in_specs = (P("group", "blk", None), P("group"), P("group", "blk", None, None)) + (P(),) * 7
    out_specs = (P("group", "blk", None), P(None, "blk", "group", None))
    return jax.shard_map(shards, mesh=mesh, in_specs=in_specs, out_specs=out_specs, check_vma=False)
```

```python
import functools, math
import jax, jax.numpy as jnp
from jax import lax
from jax.experimental import pallas as pl
from jax.experimental.pallas import tpu as pltpu
F32, BF16 = jnp.float32, jnp.bfloat16
NEG = -1e30

def prep_keys(src, row0, rows, length, kt_ref, vo_ref):
    x = src.astype(F32)
    lane = lax.broadcasted_iota(jnp.int32, x.shape, 1)
    if length is None:
        bias = jnp.zeros_like(x)
    else:
        row = lax.broadcasted_iota(jnp.int32, x.shape, 0) + row0
        bias = jnp.where(row < length, 0.0, NEG)
    k = jnp.where(lane < 64, x, bias)
    kt_ref[:, pl.ds(row0, rows)] = k.T.astype(BF16)
    vo_ref[pl.ds(row0, rows), :] = jnp.where(lane < 64, 1.0, x).astype(BF16)

def prep_q(src, qs_ref, i):
    x = src.astype(F32)
    lane = lax.broadcasted_iota(jnp.int32, x.shape, 1)
    tail = jnp.where(lane == 64, 1.0, 0.0)
    qs_ref[i, 0:256, :] = jnp.where(lane < 64, x, tail).astype(BF16)
    qs_ref[i, 256:512, :] = jnp.where(lane < 64, pltpu.roll(x, 64, 1), tail).astype(BF16)

KB = 512
def attend(qs, kt, vo, s0, s1, mx0, mx1, accs, ms, arrived, emit):
    n = 2048 // KB
    def qk(i, base, c, s, mx, diag=None, width=KB):
        off = c * KB
        sc = jnp.dot(qs[i], kt[:, base + off:base + off + width], preferred_element_type=F32)
        if diag is not None:
            r = lax.broadcasted_iota(jnp.int32, (512, width), 0)
            r = jnp.where(r >= 256, r - 256, r) + diag * 256
            col = lax.broadcasted_iota(jnp.int32, (512, width), 1)
            sc = jnp.where(col <= r, sc, NEG)
        s[:, off:off + width] = sc
        mm = sc[:, 0:128]
        for l in range(1, width // 128):
            mm = jnp.maximum(mm, sc[:, l * 128:(l + 1) * 128])
        mx[...] = jnp.maximum(mx[...], mm)
    def pv(base, c, s, mx, width=KB):
        off = c * KB
        m = mx[...]
        p = jnp.exp2(s[:, off:off + width] - jnp.concatenate([m] * (width // 128), 1)).astype(BF16)
        return jnp.dot(p, vo[base + off:base + off + width, :], preferred_element_type=F32)
    def row_max(mx):
        return jnp.broadcast_to(jnp.max(mx[...], 1, keepdims=True), mx.shape)

    def cached(inext, i, s, mx, t, tmx):
        if inext is not None:
            tmx[...] = jnp.full(tmx.shape, NEG, F32)
        tot = None
        for c in range(n):
            if inext is not None:
                qk(inext, 0, c, t, tmx)
            part = pv(0, c, s, mx)
            tot = part if tot is None else tot + part
        accs[i] = tot
        if inext is not None:
            m = row_max(tmx)
            tmx[...] = m
            ms[inext] = m
    mx0[...] = jnp.full(mx0.shape, NEG, F32)
    for c in range(n):
        qk(0, 0, c, s0, mx0)
    m = row_max(mx0)
    mx0[...] = m
    ms[0] = m
    def cached_pair(t, _):
        cached(2 * t + 1, 2 * t, s0, mx0, s1, mx1)
        cached(2 * t + 2, 2 * t + 1, s1, mx1, s0, mx0)
        return 0
    lax.fori_loop(0, 3, cached_pair, 0)
    cached(7, 6, s0, mx0, s1, mx1)
    cached(None, 7, s1, mx1, None, None)

    arrived()
    def start(i, mx):
        mx[...] = ms[i]
    def finish_max(i, mx):
        m = row_max(mx)
        mx[...] = m
        accs[i] = accs[i] * jnp.exp2(ms[i] - m)
    def out(i):
        a = accs[i]
        lane = lax.broadcasted_iota(jnp.int32, (256, 128), 1)
        h0, h1 = a[0:256], a[256:512]
        num = jnp.where(lane < 64, pltpu.roll(h0, 64, 1), h1)
        den = jnp.where(lane < 64, h0, pltpu.roll(h1, 64, 1))
        emit(i, (num / den).astype(BF16))
    def width(i, c):
        return 256 if i % 2 == 0 and c == i // 2 else KB
    def scores(i, c, s, mx):
        qk(i, 2048, c, s, mx, i % 2 if c == i // 2 else None, width(i, c))
    bufs = [(s0, mx0), (s1, mx1)]
    start(0, mx0)
    scores(0, 0, s0, mx0)
    finish_max(0, mx0)
    for i in range(8):
        s, mx = bufs[i % 2]
        t, tmx = bufs[1 - i % 2]
        if i < 7:
            start(i + 1, tmx)
        tot = accs[i]
        for c in range(min(i + 1, 7) // 2 + 1):
            if i < 7:
                scores(i + 1, c, t, tmx)
            if c <= i // 2:
                tot = tot + pv(2048, c, s, mx, width(i, c))
        accs[i] = tot
        if i < 7:
            finish_max(i + 1, tmx)
        out(i)

EPS=1e-5; THETA=1e6
QSCALE = 0.125 * math.log2(math.e)

def rope_tables(pos_f):
    lane = lax.broadcasted_iota(jnp.int32, (1, 128), 1)
    inv = jnp.exp(lax.rem(lane, 32).astype(F32) * (-2.0 / 64.0 * math.log(THETA)))
    ang = pos_f * inv
    sgn = jnp.where(lax.rem(lane, 64) < 32, -1.0, 1.0)
    return jnp.cos(ang), jnp.sin(ang) * sgn

def norm_rows(hid, gain):
    x = hid.astype(F32)
    return (x * lax.rsqrt(jnp.mean(x * x, -1, keepdims=True) + EPS) * gain).astype(BF16)

def block_ones():
    a = lax.broadcasted_iota(jnp.int32, (128, 128), 0) // 64
    b = lax.broadcasted_iota(jnp.int32, (128, 128), 1) // 64
    return jnp.where(a == b, 1.0, 0.0).astype(BF16)

def head_rope(x, gain, cos, sin, ones):
    sq = x * x
    hi = sq.astype(BF16)
    lo = (sq - hi.astype(F32)).astype(BF16)
    tot = jnp.dot(hi, ones, preferred_element_type=F32) + jnp.dot(lo, ones, preferred_element_type=F32)
    n = x * lax.rsqrt(tot * (1.0 / 64) + EPS) * gain
    lane = lax.broadcasted_iota(jnp.int32, n.shape, 1)
    sw = jnp.where(lax.rem(lane, 64) < 32, pltpu.roll(n, 96, 1), pltpu.roll(n, 32, 1))
    return n * cos + sw * sin

def pair_gain(g_ref, j):
    return jnp.concatenate([g_ref[2 * j:2 * j + 1, :], g_ref[2 * j + 1:2 * j + 2, :]], 1)

def remote(src, dst, ssem, rsem, dev):
    return pltpu.make_async_remote_copy(src_ref=src, dst_ref=dst, send_sem=ssem, recv_sem=rsem,
                                        device_id=dev, device_id_type=pl.DeviceIdType.MESH)

def layer_kernel(len_ref, hid_hbm, cache_hbm, ng_hbm, qg_hbm, kg_hbm, wk_hbm, wv_hbm, wq_hbm, wo_hbm, out_ref, dec_ref,
                 w, wo, normed, kvnew, qsend, kvc, kvn, qrecv, osend, orecv, oall, qs, kt, vo, s0, s1, mx0, mx1, accs, ms, heads,
                 hid_ref, cache_ref, ng_ref, qg_ref, kg_ref, isem, wsem, wosem, c_ss, c_rs, n_ss, n_rs, q_ss, q_rs, d_ss, d_rs, o_ss, o_rs):
    b = lax.axis_index("blk"); g = lax.axis_index("group")
    def col(n):
        return pl.ds(pl.multiple_of(n * 512, 512), 512)
    plane = [(b // 4 + 1 + c) % 4 for c in range(4)]
    copies = [pltpu.make_async_copy(wq_hbm.at[:, col(plane[c])], w.at[c], wsem.at[c]) for c in range(4)]
    copies += [pltpu.make_async_copy(wk_hbm, w.at[4], wsem.at[4]), pltpu.make_async_copy(wv_hbm, w.at[5], wsem.at[5])]
    small = [pltpu.make_async_copy(src, dst, isem.at[n]) for n, (src, dst) in enumerate(
        [(cache_hbm, cache_ref), (hid_hbm, hid_ref), (ng_hbm, ng_ref), (qg_hbm, qg_ref), (kg_hbm, kg_ref)])]
    for cp in small + copies:
        cp.start()
    barrier = pltpu.get_barrier_semaphore()
    def hello(r, _):
        pl.semaphore_signal(barrier, inc=1, device_id=((b + r) % 16, g), device_id_type=pl.DeviceIdType.MESH); return 0
    lax.fori_loop(1, 16, hello, 0)
    def hello_group(r, _):
        pl.semaphore_signal(barrier, inc=1, device_id=(b, (g + r) % 8), device_id_type=pl.DeviceIdType.MESH); return 0
    lax.fori_loop(1, 8, hello_group, 0)
    small[0].wait()
    heads[...] = jnp.swapaxes(cache_ref[...].astype(F32), 0, 1).astype(BF16)
    pl.semaphore_wait(barrier, 22)

    def c_copy(d):
        return remote(heads.at[d // 2], kvc.at[b], c_ss.at[d], c_rs.at[b], (d, g))
    def n_copy(d):
        return remote(kvnew.at[d // 2], kvn.at[b], n_ss.at[d], n_rs.at[b], (d, g))
    def q_copy(d):
        return remote(qsend.at[d], qrecv.at[b], q_ss.at[d], q_rs.at[b], (d, g))
    def d_copy(e):
        return remote(kvnew.at[e], dec_ref.at[g], d_ss.at[e], d_rs.at[g], (b, e))
    def o_copy(c):
        hi = c // 16
        return remote(osend.at[pl.ds(pl.multiple_of(c * 64, 64), 64)], orecv.at[b, pl.ds(pl.multiple_of(hi * 64, 64), 64)],
                      o_ss.at[c], o_rs.at[hi, b], (c + hi * (31 - 2 * c), g))
    def others(f):
        def body(r, _):
            f((b + r) % 16); return 0
        lax.fori_loop(1, 16, body, 0)
    def landed(buf, sem, s):
        remote(buf.at[s], buf.at[s], sem.at[s], sem.at[s], (s, g)).wait_recv()

    others(lambda d: c_copy(d).start())
    kvc[pl.ds(b, 1)] = heads[pl.ds(b // 2, 1)]

    length = len_ref[0]
    j = lax.broadcasted_iota(jnp.int32, (128, 1), 0)
    pos = jnp.where(j < 64, b * 64 + j, (31 - b) * 64 + j - 64) + length
    cos, sin = rope_tables(pos.astype(F32))
    for cp in small[1:]:
        cp.wait()
    normed[...] = norm_rows(hid_ref[...], ng_ref[...])
    ones = block_ones()
    lane = lax.broadcasted_iota(jnp.int32, (128, 128), 1)
    cosq, sinq = cos * QSCALE, sin * QSCALE
    for c in range(4):
        copies[c].wait()
        q = jnp.dot(normed[...], w[c], preferred_element_type=F32)
        for t in range(4):
            d = plane[c] * 4 + t
            gain = jnp.concatenate([qg_ref[pl.ds(2 * d, 1), :], qg_ref[pl.ds(2 * d + 1, 1), :]], 1)
            qsend[d] = head_rope(q[:, t * 128:(t + 1) * 128], gain, cosq, sinq, ones).astype(BF16)
        def send_q(t, _):
            d = plane[c] * 4 + t
            @pl.when(d != b)
            def _():
                q_copy(d).start()
            return 0
        lax.fori_loop(0, 4, send_q, 0)
    qrecv[pl.ds(b, 1)] = qsend[pl.ds(b, 1)]
    copies[4].wait(); copies[5].wait()
    k = jnp.dot(normed[...], w[4], preferred_element_type=F32)
    v = jnp.dot(normed[...], w[5], preferred_element_type=F32)
    for t in range(4):
        kk = head_rope(k[:, t * 128:(t + 1) * 128], pair_gain(kg_ref, t), cos, sin, ones)
        vv = v[:, t * 128:(t + 1) * 128]
        kvnew[2 * t] = jnp.where(lane < 64, kk, pltpu.roll(vv, 64, 1)).astype(BF16)
        kvnew[2 * t + 1] = jnp.where(lane < 64, pltpu.roll(kk, 64, 1), vv).astype(BF16)
    others(lambda d: n_copy(d).start())
    kvn[pl.ds(b, 1)] = kvnew[pl.ds(b // 2, 1)]

    wcopies = [pltpu.make_async_copy(wo_hbm.at[:, pl.ds(512 * n, 512)], wo.at[n], wosem.at[n]) for n in range(4)]
    for cp in wcopies:
        cp.start()
    def send_dec(r, _):
        d_copy((g + r) % 8).start(); return 0
    lax.fori_loop(1, 8, send_dec, 0)
    dec_ref[pl.ds(g, 1)] = kvnew[pl.ds(g, 1)]

    def cache_block(s):
        prep_keys(kvc[s], pl.multiple_of(s * 128, 128), 128, length, kt, vo)
    cache_block(b)
    def cache_in(s):
        landed(kvc, c_rs, s)
        cache_block(s)
    others(cache_in)
    others(lambda s: landed(qrecv, q_rs, s))
    def quad(i, _):
        prep_q(jnp.concatenate([qrecv[4 * i + n, 0:64] for n in range(4)], 0), qs, i)
        prep_q(jnp.concatenate([qrecv[4 * i + 3 - n, 64:128] for n in range(4)], 0), qs, 7 - i)
        return 0
    lax.fori_loop(0, 4, quad, 0)
    def arrived():
        others(lambda s: landed(kvn, n_rs, s))
        def new_pair(i, _):
            lo = jnp.concatenate([kvn[2 * i, 0:64], kvn[2 * i + 1, 0:64]], 0)
            hi = jnp.concatenate([kvn[2 * i + 1, 64:128], kvn[2 * i, 64:128]], 0)
            prep_keys(lo, pl.multiple_of(2048 + i * 128, 128), 128, None, kt, vo)
            prep_keys(hi, pl.multiple_of(2048 + (15 - i) * 128, 128), 128, None, kt, vo)
            return 0
        lax.fori_loop(0, 8, new_pair, 0)
    def emit(i, val):
        osend[pl.ds(pl.multiple_of(i * 256, 256), 256), :] = val
        def one(n, _):
            c = 4 * i + n
            hi = c // 16
            dest = c + hi * (31 - 2 * c)
            @pl.when(dest != b)
            def _():
                o_copy(c).start()
            @pl.when(dest == b)
            def _():
                orecv[b, pl.ds(pl.multiple_of(hi * 64, 64), 64), :] = osend[pl.ds(pl.multiple_of(c * 64, 64), 64), :]
            return 0
        lax.fori_loop(0, 4, one, 0)
    attend(qs, kt, vo, s0, s1, mx0, mx1, accs, ms, arrived, emit)

    def o_in(s):
        for hi in range(2):
            half = orecv.at[s, pl.ds(hi * 64, 64)]
            remote(half, half, o_ss.at[s], o_rs.at[hi, s], (s, g)).wait_recv()
    others(o_in)
    for s in range(16):
        oall[:, s * 128:(s + 1) * 128] = orecv[s]
    for n in range(4):
        wcopies[n].wait()
        out_ref[:, n * 512:(n + 1) * 512] = jnp.dot(oall[...], wo[n], preferred_element_type=F32).astype(BF16)

    def drain(d):
        c_copy(d).wait_send(); n_copy(d).wait_send(); q_copy(d).wait_send()
        o_copy(d).wait_send(); o_copy(31 - d).wait_send()
    others(drain)
    def drain_dec(r, _):
        e = (g + r) % 8
        d_copy(e).wait_send()
        remote(dec_ref.at[e], dec_ref.at[e], d_ss.at[e], d_rs.at[e], (b, e)).wait_recv()
        return 0
    lax.fori_loop(1, 8, drain_dec, 0)

def shards(hidden, cache_len, cache_kv, norm_gain, w_query, w_key, w_value, q_gain, k_gain, w_out):
    vm = pl.BlockSpec(memory_space=pltpu.VMEM); hb = pl.BlockSpec(memory_space=pltpu.HBM)
    blocks = lambda n: pltpu.VMEM((n, 128, 128), BF16)
    dma = pltpu.SemaphoreType.DMA
    out, dec = pl.pallas_call(layer_kernel,
        out_shape=(jax.ShapeDtypeStruct((128, 2048), BF16), jax.ShapeDtypeStruct((8, 128, 128), BF16)),
        in_specs=[pl.BlockSpec(memory_space=pltpu.SMEM)] + [hb] * 9, out_specs=(vm, vm),
        scratch_shapes=[pltpu.VMEM((6, 2048, 512), BF16), pltpu.VMEM((4, 2048, 512), BF16), pltpu.VMEM((128, 2048), BF16),
            blocks(8), blocks(16), blocks(16), blocks(16), blocks(16), pltpu.VMEM((2048, 128), BF16), blocks(16),
            pltpu.VMEM((128, 2048), BF16), pltpu.VMEM((8, 512, 128), BF16), pltpu.VMEM((128, 4096), BF16),
            pltpu.VMEM((4096, 128), BF16), pltpu.VMEM((512, 2048), F32), pltpu.VMEM((512, 2048), F32),
            pltpu.VMEM((512, 128), F32), pltpu.VMEM((512, 128), F32), pltpu.VMEM((8, 512, 128), F32), pltpu.VMEM((8, 512, 128), F32), blocks(8),
            pltpu.VMEM((128, 2048), BF16), pltpu.VMEM((128, 8, 128), BF16), pltpu.VMEM((1, 2048), F32),
            pltpu.VMEM((32, 64), F32), pltpu.VMEM((8, 64), F32), dma((5,)), dma((6,)), dma((4,))] + [dma((16,))] * 6 + [dma((8,))] * 2 + [dma((32,)), dma((2, 16))],
        compiler_params=pltpu.CompilerParams(vmem_limit_bytes=52 << 20, collective_id=0, has_side_effects=True),
        name="layer")(cache_len, *[pltpu.with_memory_space_constraint(x, pltpu.HBM) for x in (
            hidden[0], cache_kv[0], norm_gain[None], q_gain, k_gain, w_key, w_value, w_query, w_out)])
    return out[None], dec[:, :, None, :]


def solution(mesh):
    from jax.sharding import PartitionSpec as P
    in_specs = (P("group", "blk", None), P("group"), P("group", "blk", None, None)) + (P(),) * 7
    out_specs = (P("group", "blk", None), P(None, "blk", "group", None))
    return jax.shard_map(shards, mesh=mesh, in_specs=in_specs, out_specs=out_specs, check_vma=False)
```

```python
import functools, math
import jax, jax.numpy as jnp
from jax import lax
from jax.experimental import pallas as pl
from jax.experimental.pallas import tpu as pltpu
F32, BF16 = jnp.float32, jnp.bfloat16
NEG = -1e30

def prep_keys(src, row0, rows, length, kt_ref, vo_ref):
    x = src.astype(F32)
    lane = lax.broadcasted_iota(jnp.int32, x.shape, 1)
    if length is None:
        bias = jnp.zeros_like(x)
    else:
        row = lax.broadcasted_iota(jnp.int32, x.shape, 0) + row0
        bias = jnp.where(row < length, 0.0, NEG)
    k = jnp.where(lane < 64, x, bias)
    kt_ref[:, pl.ds(row0, rows)] = k.T.astype(BF16)
    vo_ref[pl.ds(row0, rows), :] = jnp.where(lane < 64, 1.0, x).astype(BF16)

def prep_q(src, qs_ref, i):
    x = src.astype(F32)
    lane = lax.broadcasted_iota(jnp.int32, x.shape, 1)
    tail = jnp.where(lane == 64, 1.0, 0.0)
    qs_ref[i, 0:256, :] = jnp.where(lane < 64, x, tail).astype(BF16)
    qs_ref[i, 256:512, :] = jnp.where(lane < 64, pltpu.roll(x, 64, 1), tail).astype(BF16)

KB = 512
def attend(qs, kt, vo, s0, s1, mx0, mx1, accs, ms, plane_in, arrived, emit):
    n = 2048 // KB
    def qk(i, base, c, s, mx, diag=None, width=KB):
        off = c * KB
        sc = jnp.dot(qs[i], kt[:, base + off:base + off + width], preferred_element_type=F32)
        if diag is not None:
            r = lax.broadcasted_iota(jnp.int32, (512, width), 0)
            r = jnp.where(r >= 256, r - 256, r) + diag * 256
            col = lax.broadcasted_iota(jnp.int32, (512, width), 1)
            sc = jnp.where(col <= r, sc, NEG)
        s[:, off:off + width] = sc
        mm = sc[:, 0:128]
        for l in range(1, width // 128):
            mm = jnp.maximum(mm, sc[:, l * 128:(l + 1) * 128])
        mx[...] = jnp.maximum(mx[...], mm)
    def pv(base, c, s, mx, width=KB):
        off = c * KB
        m = mx[...]
        p = jnp.exp2(s[:, off:off + width] - jnp.concatenate([m] * (width // 128), 1)).astype(BF16)
        return jnp.dot(p, vo[base + off:base + off + width, :], preferred_element_type=F32)
    def row_max(mx):
        return jnp.broadcast_to(jnp.max(mx[...], 1, keepdims=True), mx.shape)

    def cached(inext, i, s, mx, t, tmx):
        if inext is not None:
            tmx[...] = jnp.full(tmx.shape, NEG, F32)
        tot = None
        for c in range(n):
            if inext is not None:
                qk(inext, 0, c, t, tmx)
            part = pv(0, c, s, mx)
            tot = part if tot is None else tot + part
        accs[i] = tot
        if inext is not None:
            m = row_max(tmx)
            tmx[...] = m
            ms[inext] = m
    plane_in(0)
    mx0[...] = jnp.full(mx0.shape, NEG, F32)
    for c in range(n):
        qk(0, 0, c, s0, mx0)
    m = row_max(mx0)
    mx0[...] = m
    ms[0] = m
    def cached_pair(t, _):
        cached(7 - t, t, s0, mx0, s1, mx1)
        plane_in(t + 1)
        cached(t + 1, 7 - t, s1, mx1, s0, mx0)
        return 0
    lax.fori_loop(0, 3, cached_pair, 0)
    cached(4, 3, s0, mx0, s1, mx1)
    cached(None, 4, s1, mx1, None, None)

    arrived()
    def start(i, mx):
        mx[...] = ms[i]
    def finish_max(i, mx):
        m = row_max(mx)
        mx[...] = m
        accs[i] = accs[i] * jnp.exp2(ms[i] - m)
    def out(i):
        a = accs[i]
        lane = lax.broadcasted_iota(jnp.int32, (256, 128), 1)
        h0, h1 = a[0:256], a[256:512]
        num = jnp.where(lane < 64, pltpu.roll(h0, 64, 1), h1)
        den = jnp.where(lane < 64, h0, pltpu.roll(h1, 64, 1))
        emit(i, (num / den).astype(BF16))
    def width(i, c):
        return 256 if i % 2 == 0 and c == i // 2 else KB
    def scores(i, c, s, mx):
        qk(i, 2048, c, s, mx, i % 2 if c == i // 2 else None, width(i, c))
    bufs = [(s0, mx0), (s1, mx1)]
    start(0, mx0)
    scores(0, 0, s0, mx0)
    finish_max(0, mx0)
    for i in range(8):
        s, mx = bufs[i % 2]
        t, tmx = bufs[1 - i % 2]
        if i < 7:
            start(i + 1, tmx)
        tot = accs[i]
        for c in range(min(i + 1, 7) // 2 + 1):
            if i < 7:
                scores(i + 1, c, t, tmx)
            if c <= i // 2:
                tot = tot + pv(2048, c, s, mx, width(i, c))
        accs[i] = tot
        if i < 7:
            finish_max(i + 1, tmx)
        out(i)

EPS=1e-5; THETA=1e6
QSCALE = 0.125 * math.log2(math.e)

def rope_tables(pos_f):
    lane = lax.broadcasted_iota(jnp.int32, (1, 128), 1)
    inv = jnp.exp(lax.rem(lane, 32).astype(F32) * (-2.0 / 64.0 * math.log(THETA)))
    ang = pos_f * inv
    sgn = jnp.where(lax.rem(lane, 64) < 32, -1.0, 1.0)
    return jnp.cos(ang), jnp.sin(ang) * sgn

def norm_rows(hid, gain):
    x = hid.astype(F32)
    return (x * lax.rsqrt(jnp.mean(x * x, -1, keepdims=True) + EPS) * gain).astype(BF16)

def block_ones():
    a = lax.broadcasted_iota(jnp.int32, (128, 128), 0) // 64
    b = lax.broadcasted_iota(jnp.int32, (128, 128), 1) // 64
    return jnp.where(a == b, 1.0, 0.0).astype(BF16)

def head_rope(x, gain, cos, sin, ones):
    sq = x * x
    hi = sq.astype(BF16)
    lo = (sq - hi.astype(F32)).astype(BF16)
    tot = jnp.dot(hi, ones, preferred_element_type=F32) + jnp.dot(lo, ones, preferred_element_type=F32)
    n = x * lax.rsqrt(tot * (1.0 / 64) + EPS) * gain
    lane = lax.broadcasted_iota(jnp.int32, n.shape, 1)
    sw = jnp.where(lax.rem(lane, 64) < 32, pltpu.roll(n, 96, 1), pltpu.roll(n, 32, 1))
    return n * cos + sw * sin

def pair_gain(g_ref, j):
    return jnp.concatenate([g_ref[2 * j:2 * j + 1, :], g_ref[2 * j + 1:2 * j + 2, :]], 1)

def remote(src, dst, ssem, rsem, dev):
    return pltpu.make_async_remote_copy(src_ref=src, dst_ref=dst, send_sem=ssem, recv_sem=rsem,
                                        device_id=dev, device_id_type=pl.DeviceIdType.MESH)

def layer_kernel(len_ref, hid_hbm, cache_hbm, ng_hbm, qg_hbm, kg_hbm, wk_hbm, wv_hbm, wq_hbm, wo_hbm, out_ref, dec_ref,
                 w, wo, normed, kvnew, qsend, kvc, kvn, qrecv, osend, orecv, oall, qs, kt, vo, s0, s1, mx0, mx1, accs, ms, heads,
                 hid_ref, cache_ref, ng_ref, qg_ref, kg_ref, isem, wsem, wosem, c_ss, c_rs, n_ss, n_rs, q_ss, q_rs, d_ss, d_rs, o_ss, o_rs):
    b = lax.axis_index("blk"); g = lax.axis_index("group")
    def col(n):
        return pl.ds(pl.multiple_of(n * 512, 512), 512)
    plane = [(b // 4 + 1 + c) % 4 for c in range(4)]
    copies = [pltpu.make_async_copy(wq_hbm.at[:, col(plane[c])], w.at[c], wsem.at[c]) for c in range(4)]
    copies += [pltpu.make_async_copy(wk_hbm, w.at[4], wsem.at[4]), pltpu.make_async_copy(wv_hbm, w.at[5], wsem.at[5])]
    small = [pltpu.make_async_copy(src, dst, isem.at[n]) for n, (src, dst) in enumerate(
        [(cache_hbm, cache_ref), (hid_hbm, hid_ref), (ng_hbm, ng_ref), (qg_hbm, qg_ref), (kg_hbm, kg_ref)])]
    for cp in small + copies:
        cp.start()
    barrier = pltpu.get_barrier_semaphore()
    def hello(r, _):
        pl.semaphore_signal(barrier, inc=1, device_id=((b + r) % 16, g), device_id_type=pl.DeviceIdType.MESH); return 0
    lax.fori_loop(1, 16, hello, 0)
    def hello_group(r, _):
        pl.semaphore_signal(barrier, inc=1, device_id=(b, (g + r) % 8), device_id_type=pl.DeviceIdType.MESH); return 0
    lax.fori_loop(1, 8, hello_group, 0)
    small[0].wait()
    heads[...] = jnp.swapaxes(cache_ref[...].astype(F32), 0, 1).astype(BF16)
    pl.semaphore_wait(barrier, 22)

    def c_copy(d):
        return remote(heads.at[d // 2], kvc.at[b], c_ss.at[d], c_rs.at[b], (d, g))
    def n_copy(d):
        return remote(kvnew.at[d // 2], kvn.at[b], n_ss.at[d], n_rs.at[b], (d, g))
    def q_copy(d):
        return remote(qsend.at[d], qrecv.at[b], q_ss.at[d], q_rs.at[b], (d, g))
    def d_copy(e):
        return remote(kvnew.at[e], dec_ref.at[g], d_ss.at[e], d_rs.at[g], (b, e))
    def o_copy(c):
        hi = c // 16
        return remote(osend.at[pl.ds(pl.multiple_of(c * 64, 64), 64)], orecv.at[b, pl.ds(pl.multiple_of(hi * 64, 64), 64)],
                      o_ss.at[c], o_rs.at[hi, b], (c + hi * (31 - 2 * c), g))
    def others(f):
        def body(r, _):
            f((b + r) % 16); return 0
        lax.fori_loop(1, 16, body, 0)
    def landed(buf, sem, s):
        remote(buf.at[s], buf.at[s], sem.at[s], sem.at[s], (s, g)).wait_recv()

    others(lambda d: c_copy(d).start())
    kvc[pl.ds(b, 1)] = heads[pl.ds(b // 2, 1)]

    length = len_ref[0]
    j = lax.broadcasted_iota(jnp.int32, (128, 1), 0)
    pos = jnp.where(j < 64, b * 64 + j, (31 - b) * 64 + j - 64) + length
    cos, sin = rope_tables(pos.astype(F32))
    for cp in small[1:]:
        cp.wait()
    normed[...] = norm_rows(hid_ref[...], ng_ref[...])
    ones = block_ones()
    lane = lax.broadcasted_iota(jnp.int32, (128, 128), 1)
    cosq, sinq = cos * QSCALE, sin * QSCALE
    for c in range(4):
        copies[c].wait()
        q = jnp.dot(normed[...], w[c], preferred_element_type=F32)
        for t in range(4):
            d = plane[c] * 4 + t
            gain = jnp.concatenate([qg_ref[pl.ds(2 * d, 1), :], qg_ref[pl.ds(2 * d + 1, 1), :]], 1)
            qsend[d] = head_rope(q[:, t * 128:(t + 1) * 128], gain, cosq, sinq, ones).astype(BF16)
        def send_q(t, _):
            d = plane[c] * 4 + t
            @pl.when(d != b)
            def _():
                q_copy(d).start()
            return 0
        lax.fori_loop(0, 4, send_q, 0)
    qrecv[pl.ds(b, 1)] = qsend[pl.ds(b, 1)]
    copies[4].wait(); copies[5].wait()
    k = jnp.dot(normed[...], w[4], preferred_element_type=F32)
    v = jnp.dot(normed[...], w[5], preferred_element_type=F32)
    for t in range(4):
        kk = head_rope(k[:, t * 128:(t + 1) * 128], pair_gain(kg_ref, t), cos, sin, ones)
        vv = v[:, t * 128:(t + 1) * 128]
        kvnew[2 * t] = jnp.where(lane < 64, kk, pltpu.roll(vv, 64, 1)).astype(BF16)
        kvnew[2 * t + 1] = jnp.where(lane < 64, pltpu.roll(kk, 64, 1), vv).astype(BF16)
    others(lambda d: n_copy(d).start())
    kvn[pl.ds(b, 1)] = kvnew[pl.ds(b // 2, 1)]

    wcopies = [pltpu.make_async_copy(wo_hbm.at[:, pl.ds(512 * n, 512)], wo.at[n], wosem.at[n]) for n in range(4)]
    for cp in wcopies:
        cp.start()
    def send_dec(r, _):
        d_copy((g + r) % 8).start(); return 0
    lax.fori_loop(1, 8, send_dec, 0)
    dec_ref[pl.ds(g, 1)] = kvnew[pl.ds(g, 1)]

    def cache_block(s):
        prep_keys(kvc[s], pl.multiple_of(s * 128, 128), 128, length, kt, vo)
    cache_block(b)
    def cache_in(s):
        landed(kvc, c_rs, s)
        cache_block(s)
    others(cache_in)
    def plane_in(i):
        def wait_q(n, _):
            @pl.when(4 * i + n != b)
            def _():
                landed(qrecv, q_rs, 4 * i + n)
            return 0
        lax.fori_loop(0, 4, wait_q, 0)
        prep_q(jnp.concatenate([qrecv[4 * i + n, 0:64] for n in range(4)], 0), qs, i)
        prep_q(jnp.concatenate([qrecv[4 * i + 3 - n, 64:128] for n in range(4)], 0), qs, 7 - i)
    def arrived():
        others(lambda s: landed(kvn, n_rs, s))
        def new_pair(i, _):
            lo = jnp.concatenate([kvn[2 * i, 0:64], kvn[2 * i + 1, 0:64]], 0)
            hi = jnp.concatenate([kvn[2 * i + 1, 64:128], kvn[2 * i, 64:128]], 0)
            prep_keys(lo, pl.multiple_of(2048 + i * 128, 128), 128, None, kt, vo)
            prep_keys(hi, pl.multiple_of(2048 + (15 - i) * 128, 128), 128, None, kt, vo)
            return 0
        lax.fori_loop(0, 8, new_pair, 0)
    def emit(i, val):
        osend[pl.ds(pl.multiple_of(i * 256, 256), 256), :] = val
        def one(n, _):
            c = 4 * i + n
            hi = c // 16
            dest = c + hi * (31 - 2 * c)
            @pl.when(dest != b)
            def _():
                o_copy(c).start()
            @pl.when(dest == b)
            def _():
                orecv[b, pl.ds(pl.multiple_of(hi * 64, 64), 64), :] = osend[pl.ds(pl.multiple_of(c * 64, 64), 64), :]
            return 0
        lax.fori_loop(0, 4, one, 0)
    attend(qs, kt, vo, s0, s1, mx0, mx1, accs, ms, plane_in, arrived, emit)

    def o_in(s):
        for hi in range(2):
            half = orecv.at[s, pl.ds(hi * 64, 64)]
            remote(half, half, o_ss.at[s], o_rs.at[hi, s], (s, g)).wait_recv()
    others(o_in)
    for s in range(16):
        oall[:, s * 128:(s + 1) * 128] = orecv[s]
    for n in range(4):
        wcopies[n].wait()
        out_ref[:, n * 512:(n + 1) * 512] = jnp.dot(oall[...], wo[n], preferred_element_type=F32).astype(BF16)

    def drain(d):
        c_copy(d).wait_send(); n_copy(d).wait_send(); q_copy(d).wait_send()
        o_copy(d).wait_send(); o_copy(31 - d).wait_send()
    others(drain)
    def drain_dec(r, _):
        e = (g + r) % 8
        d_copy(e).wait_send()
        remote(dec_ref.at[e], dec_ref.at[e], d_ss.at[e], d_rs.at[e], (b, e)).wait_recv()
        return 0
    lax.fori_loop(1, 8, drain_dec, 0)

def shards(hidden, cache_len, cache_kv, norm_gain, w_query, w_key, w_value, q_gain, k_gain, w_out):
    vm = pl.BlockSpec(memory_space=pltpu.VMEM); hb = pl.BlockSpec(memory_space=pltpu.HBM)
    blocks = lambda n: pltpu.VMEM((n, 128, 128), BF16)
    dma = pltpu.SemaphoreType.DMA
    out, dec = pl.pallas_call(layer_kernel,
        out_shape=(jax.ShapeDtypeStruct((128, 2048), BF16), jax.ShapeDtypeStruct((8, 128, 128), BF16)),
        in_specs=[pl.BlockSpec(memory_space=pltpu.SMEM)] + [hb] * 9, out_specs=(vm, vm),
        scratch_shapes=[pltpu.VMEM((6, 2048, 512), BF16), pltpu.VMEM((4, 2048, 512), BF16), pltpu.VMEM((128, 2048), BF16),
            blocks(8), blocks(16), blocks(16), blocks(16), blocks(16), pltpu.VMEM((2048, 128), BF16), blocks(16),
            pltpu.VMEM((128, 2048), BF16), pltpu.VMEM((8, 512, 128), BF16), pltpu.VMEM((128, 4096), BF16),
            pltpu.VMEM((4096, 128), BF16), pltpu.VMEM((512, 2048), F32), pltpu.VMEM((512, 2048), F32),
            pltpu.VMEM((512, 128), F32), pltpu.VMEM((512, 128), F32), pltpu.VMEM((8, 512, 128), F32), pltpu.VMEM((8, 512, 128), F32), blocks(8),
            pltpu.VMEM((128, 2048), BF16), pltpu.VMEM((128, 8, 128), BF16), pltpu.VMEM((1, 2048), F32),
            pltpu.VMEM((32, 64), F32), pltpu.VMEM((8, 64), F32), dma((5,)), dma((6,)), dma((4,))] + [dma((16,))] * 6 + [dma((8,))] * 2 + [dma((32,)), dma((2, 16))],
        compiler_params=pltpu.CompilerParams(vmem_limit_bytes=52 << 20, collective_id=0, has_side_effects=True),
        name="layer")(cache_len, *[pltpu.with_memory_space_constraint(x, pltpu.HBM) for x in (
            hidden[0], cache_kv[0], norm_gain[None], q_gain, k_gain, w_key, w_value, w_query, w_out)])
    return out[None], dec[:, :, None, :]


def solution(mesh):
    from jax.sharding import PartitionSpec as P
    in_specs = (P("group", "blk", None), P("group"), P("group", "blk", None, None)) + (P(),) * 7
    out_specs = (P("group", "blk", None), P(None, "blk", "group", None))
    return jax.shard_map(shards, mesh=mesh, in_specs=in_specs, out_specs=out_specs, check_vma=False)
```
